256 devices in a mesh: comp: 4 (over y), horiz: 16 (over x_lo, z), trc: 4 (over x_hi, core).
Axes of the slice: x: 4 (x_hi: 2, x_lo: 2; x = x_hi * 2 + x_lo), y: 4, z: 8, core: 2. Of those that a mesh axis runs over, the one named last changes fastest.
Arguments:
- tracers: float32 [16, 64, 512, 256], P(('comp', 'trc'), None, 'horiz'), may hold values from -6 to 6
- eastward: float32 [64, 512, 256], P(('comp', 'trc'), 'horiz'), may hold values from -1.2 to 1.2
- northward: float32 [64, 512, 256], P(('comp', 'trc'), 'horiz'), may hold values from -1.2 to 1.2
- surface_height: float32 [512, 256], P('horiz'), may hold values from -6 to 6
- sea_mask: int32 [512, 256], P('horiz'), may hold values 0 or 1
- mixing: float32 [64, 512, 256], P(('comp', 'trc'), 'horiz'), may hold values from 0.02 to 0.15
- sunlight: float32 [512, 256], P('horiz'), may hold values from 0.5 to 4
- reaction: float32 [16, 16], replicated, may hold values from -1.5 to 1.5
Outputs:
- east_out: float32 [64, 512, 256], P(('comp', 'trc'), 'horiz')
- north_out: float32 [64, 512, 256], P(('comp', 'trc'), 'horiz')
- tracers_out: float32 [16, 64, 512, 256], P(None, ('comp', 'trc'), 'horiz')
- heating: float32 [64, 512, 256], P(('comp', 'trc'), 'horiz')
The draws below stay inside these ranges and needn't reach their ends.
All inputs are finite; a program needn't handle non-finite values. No bound on the sum of `sea_mask` on one device may be relied on, other than what follows from the above.
Results may differ from the reference program's by a relative error of at most 0.00017.
Values sent between devices are 32-bit elements; how exact they have to be, the bound alone decides.
No kernel may reach another device: no remote copies, remote signals or barrier semaphores. Data moves between devices by JAX's collectives and lax.ppermute only.
A program may use at most 64 MiB of HBM per device.

```python
import math
import jax
import jax.numpy as jnp
from jax import lax

NTR = 16
Y = 256
SUBSTEPS = 4
X = 512
LEVELS = 64


def set_ends(values, rng, least, largest):
    longest = values.shape.index(max(values.shape))
    spots = []
    for shift in (0, 1):
        where = [jax.random.randint(jax.random.fold_in(rng, axis), (), 0, length) for axis, length in enumerate(values.shape)]
        where[longest] = (where[longest] + shift) % values.shape[longest]
        spots.append(tuple(where))
    return values.at[spots[0]].set(least).at[spots[1]].set(largest)


def steps_of(stream_key, extent, split, least, high):
    def one(dim, blocks):
        draws = jax.random.uniform(jax.random.fold_in(jax.random.fold_in(stream_key, 6), dim), (blocks,), jnp.float32, least / len(split), high / len(split))
        return jnp.repeat(jnp.exp(draws), extent[dim] // blocks).reshape((-1,) + (1,) * (len(extent) - dim - 1))

    factor_of = one(*split[0])
    for cut in split[1:]:
        factor_of = factor_of * one(*cut)
    return factor_of


def bell_draw(stream_key, shape, deviation, most, shards=(), kind=jnp.bfloat16):
    drawn = jax.random.normal(stream_key, shape, jnp.float32) * deviation
    if len(shards) > 0:
        drawn = steps_of(stream_key, shape, shards, -0.22, 0.18) * drawn
    return jnp.clip(drawn, min=-most, max=most).astype(kind)


def setup_inputs(seed: int = 0) -> dict:
    seeds = jax.random.split(jax.random.key(seed), 9)
    tracers = bell_draw(seeds[0], (NTR, LEVELS, X, Y), 1.0, 6.0, ((0, 16), (2, 16)), jnp.float32)
    eastward = bell_draw(seeds[1], (LEVELS, X, Y), 0.4, 1.2, ((0, 16), (1, 16)), jnp.float32)
    northward = bell_draw(seeds[2], (LEVELS, X, Y), 0.4, 1.2, ((0, 16), (1, 16)), jnp.float32)
    surface_height = bell_draw(seeds[3], (X, Y), 1.0, 6.0, ((0, 16),), jnp.float32)
    sea_mask = set_ends((jax.random.randint(seeds[4], (X, Y), 0, 5) < 4).astype(jnp.int32), jax.random.fold_in(seeds[4], 1), 0, 1)
    mixing = jnp.clip(jnp.exp(math.log(0.15) - 2.014903 * jax.random.uniform(seeds[5], (LEVELS, X, Y), jnp.float32) ** steps_of(seeds[5], (LEVELS, X, Y), ((0, 16), (1, 16)), -0.2, 0.2)), 0.02, 0.15)
    sunlight = jnp.clip(jnp.exp(math.log(4.0) - 2.0794415 * jax.random.uniform(seeds[6], (X, Y), jnp.float32) ** steps_of(seeds[6], (X, Y), ((0, 16),), -0.2, 0.2)), 0.5, 4.0)
    reaction = bell_draw(seeds[7], (NTR, NTR), NTR ** -0.5, 1.5, (), jnp.float32)
    return dict(tracers=tracers, eastward=eastward, northward=northward, surface_height=surface_height, sea_mask=sea_mask, mixing=mixing, sunlight=sunlight, reaction=reaction)


TIME_STEP = 0.25
GRAVITY = 1.0
VISCOSITY = 0.05
COURANT = 0.2
HALF_LIGHT = 0.3


def pad_rows(array):
    return jnp.pad(array, [(0, 0)] * (array.ndim - 1) + [(1, 1)])


def ocean_step(east_ext, north_ext, height_ext, wet_ext, mixing, bottom_keep):
    width = east_ext.shape[1] - 4
    rows = east_ext.shape[2]
    coriolis = 0.5 + 0.5 * jnp.arange(rows, dtype=jnp.float32) / rows
    east_pad = pad_rows(east_ext)
    north_pad = pad_rows(north_ext)
    height_pad = pad_rows(height_ext)
    wet_pad = pad_rows(wet_ext)
    east_mid = east_ext[:, 1:width + 2]
    east_lap = (east_ext[:, 2:width + 3] + east_ext[:, 0:width + 1] + east_pad[:, 1:width + 2, 2:]
                + east_pad[:, 1:width + 2, :-2] - 4.0 * east_mid)
    north_avg = 0.25 * (north_pad[:, 1:width + 2, 1:-1] + north_pad[:, 2:width + 3, 1:-1]
                        + north_pad[:, 1:width + 2, :-2] + north_pad[:, 2:width + 3, :-2])
    slope_x = height_ext[2:width + 3] - height_ext[1:width + 2]
    open_x = wet_ext[1:width + 2] * wet_ext[2:width + 3]
    east_new = open_x * (east_mid + TIME_STEP * (coriolis * north_avg - GRAVITY * slope_x + VISCOSITY * east_lap))
    north_mid = north_ext[:, 2:width + 2]
    north_lap = (north_ext[:, 3:width + 3] + north_ext[:, 1:width + 1] + north_pad[:, 2:width + 2, 2:]
                 + north_pad[:, 2:width + 2, :-2] - 4.0 * north_mid)
    east_avg = 0.25 * (east_pad[:, 2:width + 2, 1:-1] + east_pad[:, 1:width + 1, 1:-1]
                       + east_pad[:, 2:width + 2, 2:] + east_pad[:, 1:width + 1, 2:])
    slope_y = height_pad[2:width + 2, 2:] - height_pad[2:width + 2, 1:-1]
    open_y = wet_pad[2:width + 2, 1:-1] * wet_pad[2:width + 2, 2:]
    north_new = open_y * (north_mid + TIME_STEP * (-coriolis * east_avg - GRAVITY * slope_y + VISCOSITY * north_lap))
    east_out = east_new[:, 1:]
    speed = jnp.minimum(east_out * east_out + north_new * north_new, 1.0)
    kappa = wet_ext[2:width + 2] * mixing * (1.0 + speed) * bottom_keep
    return east_out, north_new, COURANT * east_new, COURANT * north_new, kappa


def advance(padded, flux_x, flux_y, kappa, kappa_up):
    inner = padded[..., 1:-1, 1:-1, :]
    level_mid = padded[..., 1:-1, :, :]
    width = inner.shape[-2]
    east_flux = (jnp.maximum(flux_x, 0.0) * level_mid[..., 0:width + 1, :]
                 + jnp.minimum(flux_x, 0.0) * level_mid[..., 1:width + 2, :])
    across_x = east_flux[..., :-1, :] - east_flux[..., 1:, :]
    north_cells = jnp.pad(inner[..., 1:], [(0, 0)] * (inner.ndim - 1) + [(0, 1)])
    north_flux = jnp.maximum(flux_y, 0.0) * inner + jnp.minimum(flux_y, 0.0) * north_cells
    south_flux = jnp.pad(north_flux[..., :-1], [(0, 0)] * (inner.ndim - 1) + [(1, 0)])
    across_y = south_flux - north_flux
    below = kappa * (padded[..., 2:, 1:-1, :] - inner)
    above = kappa_up * (inner - padded[..., :-2, 1:-1, :])
    return inner + across_x + across_y + below - above


def reference(tracers, eastward, northward, surface_height, sea_mask, mixing, sunlight, reaction):
    levels = eastward.shape[0]
    wet = sea_mask.astype(jnp.float32)
    xpad = ((0, 0), (2, 2), (0, 0))
    keep = (jnp.arange(levels) < levels - 1).astype(jnp.float32)[:, None, None]
    east_out, north_out, flux_x, flux_y, kappa = ocean_step(
        jnp.pad(eastward, xpad), jnp.pad(northward, xpad),
        jnp.pad(surface_height, ((2, 2), (0, 0))), jnp.pad(wet, ((2, 2), (0, 0))), mixing, keep)
    kappa_up = jnp.pad(kappa[:-1], ((1, 0), (0, 0), (0, 0)))

    def transport(field):
        for step in range(SUBSTEPS):
            padded = jnp.pad(field, ((1, 1), (1, 1), (0, 0)))
            field = advance(padded, flux_x, flux_y, kappa, kappa_up)
        return field

    moved = lax.map(transport, tracers)
    tau = (0.5 + moved[0] * moved[0]) / levels
    depth_top = jnp.cumsum(tau, 0) - tau
    light_top = sunlight * jnp.exp(-depth_top)
    heating = levels * light_top * (1.0 - jnp.exp(-tau))
    light_mid = light_top * jnp.exp(-0.5 * tau)
    limit = light_mid / (light_mid + HALF_LIGHT)
    growth = jnp.einsum("ij,jlxy->ilxy", reaction, moved, precision=lax.Precision.HIGHEST)
    tracers_out = moved + limit * growth
    return east_out, north_out, tracers_out, heating
```

```python
import functools

import jax
import jax.numpy as jnp
from jax import lax
from jax.experimental import pallas as pl
from jax.experimental.pallas import tpu as pltpu
from jax.sharding import PartitionSpec as P

SUBSTEPS = 4
TIME_STEP = 0.25
VISCOSITY = 0.05
COURANT = 0.2
HALF_LIGHT = 0.3

HALO = 4
SHIFTS = (0, 1, 3, 2)

ANY = pl.BlockSpec(memory_space=pl.ANY)
SMEM = pl.BlockSpec(memory_space=pltpu.SMEM)
VMEM = pl.BlockSpec(memory_space=pltpu.VMEM)


def roll(x, shift, axis):
    return pltpu.roll(x, shift % x.shape[axis], axis)


def ocean_kernel(last, levels_ref, u_ref, v_ref, k_ref, h_ref, m_ref, lo_ref, hi_ref, east_ref, north_ref, flux_ref):
    depth, width, rows = u_ref.shape

    def circular(inner, index):
        return jnp.concatenate([inner, hi_ref[index], lo_ref[index]], 0)

    span = width + 16
    lane = lax.broadcasted_iota(jnp.int32, (span, rows), 1)
    first, final = lane == 0, lane == rows - 1
    east = lambda x: roll(x, -1, 0)
    west = lambda x: roll(x, 1, 0)
    north = lambda x: jnp.where(final, 0.0, roll(x, -1, 1))
    south = lambda x: jnp.where(first, 0.0, roll(x, 1, 1))
    coriolis = 0.5 + 0.5 * lane.astype(jnp.float32) / rows
    h = circular(h_ref[...], 3 * depth)
    wet = circular(m_ref[...].astype(jnp.float32), 3 * depth + 1)
    slope_x = east(h) - h
    slope_y = north(h) - h
    open_x = wet * east(wet)
    open_y = wet * north(wet)
    upper = lax.broadcasted_iota(jnp.int32, (8, rows), 0) < HALO

    def emit(index, level, x):
        flux_ref[index, level, :width, :] = x[:width]
        flux_ref[index, level, width:, :] = jnp.where(upper, x[width : width + 8], x[width + 8 :])

    for level in range(depth):
        u = circular(u_ref[level], level)
        v = circular(v_ref[level], depth + level)
        mixing = circular(k_ref[level], 2 * depth + level)
        lap = east(u) + west(u) + north(u) + south(u) - 4.0 * u
        pair = v + east(v)
        avg = 0.25 * (pair + south(pair))
        east_new = open_x * (u + TIME_STEP * (coriolis * avg - slope_x + VISCOSITY * lap))
        lap = east(v) + west(v) + north(v) + south(v) - 4.0 * v
        pair = u + west(u)
        avg = 0.25 * (pair + north(pair))
        north_new = open_y * (v + TIME_STEP * (-coriolis * avg - slope_y + VISCOSITY * lap))
        speed = jnp.minimum(east_new * east_new + north_new * north_new, 1.0)
        keep = jnp.where(levels_ref[0] + level < last, 1.0, 0.0)
        kappa = wet * mixing * (1.0 + speed) * keep
        east_ref[level] = east_new[:width]
        north_ref[level] = north_new[:width]
        emit(0, level, COURANT * east_new)
        emit(1, level, COURANT * north_new)
        emit(2, level, kappa)


def transport_kernel(levels, place_ref, inner_hbm, halo_hbm, flux_hbm, mine_ref, other_ref, send_ref, sums_ref, flux, a, b, sem):
    width = inner_hbm.shape[1]
    copies = [
        pltpu.make_async_copy(flux_hbm.at[place_ref[i]], flux.at[i], sem.at[i]) for i in range(6)
    ]
    copies.append(pltpu.make_async_copy(inner_hbm, a.at[:, :width, :], sem.at[6]))
    copies.append(pltpu.make_async_copy(halo_hbm, a.at[:, width:, :], sem.at[7]))
    for copy in copies:
        copy.start()
    for copy in copies:
        copy.wait()
    total = a.shape[0]

    def down(src, level):
        block, sub = level // HALO, level % HALO
        return flux[block, 2, sub] * (src[level + 1] - src[level])

    for step in range(SUBSTEPS):
        src, dst = (a, b) if step % 2 == 0 else (b, a)
        start, stop = step + 1, total - 1 - step

        def body(level, above, src=src, dst=dst):
            block, sub = level // HALO, level % HALO
            c = src[level]
            fx = flux[block, 0, sub]
            fy = flux[block, 1, sub]
            flow_x = fx * jnp.where(fx > 0.0, c, roll(c, -1, 0))
            flow_y = fy * jnp.where(fy > 0.0, c, roll(c, -1, 1))
            below = flux[block, 2, sub] * (src[level + 1] - c)
            dst[level] = (
                c
                + (roll(flow_x, 1, 0) - flow_x)
                + (roll(flow_y, 1, 1) - flow_y)
                + (below - above)
            )
            return below

        lax.fori_loop(start, stop, body, down(src, start - 1))
    result = b if SUBSTEPS % 2 else a
    own, opposite = place_ref[6], place_ref[7]

    def block_of(index):
        return result[pl.ds(HALO + index * HALO, HALO), :width, :]

    mine_ref[...] = block_of(own)
    other_ref[...] = block_of(own ^ 1)
    send_ref[:HALO] = block_of(opposite)
    send_ref[HALO:] = block_of(opposite ^ 1)
    for index in range(4):
        m = block_of(index)
        sums_ref[index] = jnp.sum((0.5 + m * m) / levels, 0)


def reaction_kernel(levels, order_ref, react_ref, sun_ref, start_ref, *refs):
    mine = refs[0:4]
    across = refs[4:8]
    core_ref, out_ref, heat_ref, depth, field = refs[8:]
    rows = out_ref.shape[2]
    count = out_ref.shape[0]

    @pl.when(pl.program_id(0) == 0)
    def _():
        depth[...] = jnp.sum(start_ref[...], 0)

    for slot in range(4):
        field[order_ref[slot]] = mine[slot][0]
        field[order_ref[4 + slot]] = across[slot][0]
        field[order_ref[8 + slot]] = core_ref[slot, 0]
        field[order_ref[12 + slot]] = core_ref[4 + slot, 0]

    def chunk(index, carry):
        row = pl.ds(pl.multiple_of(index * 8, 8), 8)
        m = [field[j, row, :] for j in range(count)]
        tau = (0.5 + m[0] * m[0]) / levels
        above = depth[row, :]
        light_top = sun_ref[row, :] * jnp.exp(-above)
        heat_ref[0, row, :] = levels * light_top * (1.0 - jnp.exp(-tau))
        depth[row, :] = above + tau
        light_mid = light_top * jnp.exp(-0.5 * tau)
        limit = light_mid / (light_mid + HALF_LIGHT)
        for i in range(count):
            growth = react_ref[i, 0] * m[0]
            for j in range(1, count):
                growth = growth + react_ref[i, j] * m[j]
            out_ref[i, 0, row, :] = m[i] + limit * growth
        return carry

    lax.fori_loop(0, rows // 8, chunk, 0)


def per_device(tracers, eastward, northward, surface_height, sea_mask, mixing, sunlight, reaction):
    f32 = jnp.float32
    depth, width, rows = eastward.shape
    comps, trcs = lax.axis_size("comp"), lax.axis_size("trc")
    tiles = lax.axis_size("horiz")
    levels = depth * comps * trcs
    group = depth * trcs
    c, t = lax.axis_index("comp"), lax.axis_index("trc")
    forward = [(i, i + 1) for i in range(tiles - 1)]
    backward = [(i + 1, i) for i in range(tiles - 1)]
    flip_x = [(i, i ^ 2) for i in range(trcs)]
    flip_core = [(i, i ^ 1) for i in range(trcs)]

    def ring(shift):
        return [(i, (i + shift) % comps) for i in range(comps)]

    field = tracers[0]
    padded = jnp.pad(field, ((HALO, HALO), (0, 0), (0, 0)))

    def segment(array, shift):
        return lax.dynamic_slice_in_dim(array, group * ((c + shift) % comps), group + 2 * HALO, 0)

    inner = {0: segment(padded, 0)}
    for shift in (1, 3):
        inner[shift] = lax.ppermute(segment(padded, shift), "comp", ring(shift))

    edge = jnp.concatenate(
        [eastward, northward, mixing, surface_height[None], sea_mask.astype(f32)[None]], 0
    )
    low = lax.ppermute(edge[:, width - 8 :], "horiz", forward)
    high = lax.ppermute(edge[:, :8], "horiz", backward)
    side_low = lax.ppermute(field[:, width - HALO :], "horiz", forward)
    side_high = lax.ppermute(field[:, :HALO], "horiz", backward)

    first_level = ((c * trcs + t) * depth).astype(jnp.int32)[None]
    span = width + 2 * HALO
    east_out, north_out, flux = pl.pallas_call(
        functools.partial(ocean_kernel, levels - 1),
        out_shape=(
            jax.ShapeDtypeStruct((depth, width, rows), f32),
            jax.ShapeDtypeStruct((depth, width, rows), f32),
            jax.ShapeDtypeStruct((3, depth, span, rows), f32),
        ),
        in_specs=[SMEM] + [VMEM] * 7,
        out_specs=(VMEM,) * 3,
        name="ocean",
        cost_estimate=pl.CostEstimate(flops=8_000_000, bytes_accessed=1_700_000, transcendentals=0),
    )(first_level, eastward, northward, mixing, surface_height, sea_mask, low, high)

    both = ("comp", "trc")
    flux_x = lax.ppermute(flux, "trc", flip_x)
    ups = range(comps - 1)
    near = lax.ppermute(
        flux, both, [(4 * i + 3, 4 * i + 6) for i in ups] + [(4 * i + 4, 4 * i + 1) for i in ups]
    )
    far = lax.ppermute(
        flux, both, [(4 * i + 3, 4 * i + 4) for i in ups] + [(4 * i + 4, 4 * i + 3) for i in ups]
    )
    rim = near + far
    held = jnp.stack([flux, flux_x, rim])
    theirs = lax.ppermute(held, "trc", flip_core)
    flux_all = jnp.concatenate([held, theirs], 0)
    core = t % 2
    block = jnp.arange(4)
    between = (block ^ t).astype(jnp.int32)
    inside = jnp.where(between % 2 == 1, 3, 0) + between // 2
    place = jnp.concatenate(
        [
            jnp.where(core == 0, 2, 5)[None],
            inside,
            jnp.where(core == 0, 5, 2)[None],
            t[None],
            (t ^ 2)[None],
        ]
    ).astype(jnp.int32)

    side = jnp.pad(
        jnp.concatenate([side_high, side_low], 1), ((HALO, HALO), (0, 0), (0, 0))
    )
    sides = {0: segment(side, 0)}
    for shift in (1, 3):
        sides[shift] = lax.ppermute(segment(side, shift), "comp", ring(shift))
    inner[2] = lax.ppermute(segment(padded, 2), "comp", ring(2))
    sides[2] = lax.ppermute(segment(side, 2), "comp", ring(2))

    piece = jax.ShapeDtypeStruct((depth, width, rows), f32)
    transport = pl.pallas_call(
        functools.partial(transport_kernel, levels),
        out_shape=(piece, piece, jax.ShapeDtypeStruct((2 * depth, width, rows), f32), piece),
        in_specs=[SMEM, ANY, ANY, ANY],
        out_specs=(VMEM,) * 4,
        scratch_shapes=[
            pltpu.VMEM((6, 3, depth, span, rows), f32),
            pltpu.VMEM((group + 2 * HALO, span, rows), f32),
            pltpu.VMEM((group + 2 * HALO, span, rows), f32),
            pltpu.SemaphoreType.DMA((8,)),
        ],
        name="transport",
        cost_estimate=pl.CostEstimate(flops=20_000_000, bytes_accessed=5_000_000, transcendentals=0),
    )
    mine, other, across, sums = [], [], [], []
    for shift in SHIFTS:
        m, o, s, total = transport(place, inner[shift], sides[shift], flux_all)
        mine.append(m)
        other.append(o)
        across.append(lax.ppermute(s, "trc", flip_x))
        sums.append(total)
    cross = jnp.stack(other + [a[depth:] for a in across])
    cross = lax.ppermute(cross, "trc", flip_core)

    first = jnp.where(c == 0, sums[0], jnp.where(c == 1, sums[1], jnp.where(c == 3, sums[2], sums[3])))
    first = jnp.where(t == 0, first, 0.0)
    running = [jnp.zeros_like(first[0])]
    for index in range(trcs):
        running.append(running[-1] + first[index])
    whole = running.pop()
    parts = []
    for target in range(comps):
        for index in range(trcs):
            parts.append(jnp.where(c < target, whole, jnp.where(c == target, running[index], 0.0)))
    starts = lax.all_to_all(jnp.stack(parts), both, 0, 0, tiled=True)

    home = [4 * ((c - shift) % comps) for shift in SHIFTS]
    order = jnp.stack([h + (t ^ k) for k in (0, 2, 1, 3) for h in home]).astype(jnp.int32)
    count = reaction.shape[0]
    level_block = pl.BlockSpec((1, width, rows), lambda l: (l, 0, 0))
    tracers_out, heating = pl.pallas_call(
        functools.partial(reaction_kernel, levels),
        grid=(depth,),
        out_shape=(jax.ShapeDtypeStruct((count, depth, width, rows), f32), piece),
        in_specs=[SMEM, SMEM, VMEM, VMEM]
        + [level_block] * 8
        + [pl.BlockSpec((8, 1, width, rows), lambda l: (0, l, 0, 0))],
        out_specs=(pl.BlockSpec((count, 1, width, rows), lambda l: (0, l, 0, 0)), level_block),
        scratch_shapes=[pltpu.VMEM((width, rows), f32), pltpu.VMEM((count, width, rows), f32)],
        name="reaction",
        cost_estimate=pl.CostEstimate(flops=20_000_000, bytes_accessed=5_000_000, transcendentals=100_000),
    )(order, reaction, sunlight, starts, *mine, *across, cross)
    return (east_out, north_out, tracers_out, heating)


def solution(mesh):
    return jax.shard_map(
        per_device,
        mesh=mesh,
        in_specs=(
            P(("comp", "trc"), None, "horiz", None),
            P(("comp", "trc"), "horiz", None),
            P(("comp", "trc"), "horiz", None),
            P("horiz", None),
            P("horiz", None),
            P(("comp", "trc"), "horiz", None),
            P("horiz", None),
            P(),
        ),
        out_specs=(
            P(("comp", "trc"), "horiz", None),
            P(("comp", "trc"), "horiz", None),
            P(None, ("comp", "trc"), "horiz", None),
            P(("comp", "trc"), "horiz", None),
        ),
        check_vma=False,
    )
```

```python
import functools

import jax
import jax.numpy as jnp
from jax import lax
from jax.experimental import pallas as pl
from jax.experimental.pallas import tpu as pltpu
from jax.sharding import PartitionSpec as P


SUBSTEPS = 4
TIME_STEP = 0.25
VISCOSITY = 0.05
COURANT = 0.2
HALF_LIGHT = 0.3

SHIFTS = (0, 1, 3, 2)
HALO = 4


SMEM = pl.BlockSpec(memory_space=pltpu.SMEM)
VMEM = pl.BlockSpec(memory_space=pltpu.VMEM)
ANY = pl.BlockSpec(memory_space=pl.ANY)


def local(*shape):
    return pltpu.VMEM(shape, jnp.float32)


def array(*shape):
    return jax.ShapeDtypeStruct(shape, jnp.float32)


def call(kernel, cost, **kwargs):
    return pl.pallas_call(
        kernel,
        compiler_params=pltpu.CompilerParams(vmem_limit_bytes=12 << 20),
        cost_estimate=pl.CostEstimate(flops=cost * 1_000_000, bytes_accessed=cost * 1_000_000, transcendentals=0),
        **kwargs,
    )


def in_hbm(*arrays):
    return [pltpu.with_memory_space_constraint(x, pltpu.HBM) for x in arrays]


def in_vmem(*arrays):
    return [pltpu.with_memory_space_constraint(x, pltpu.VMEM) for x in arrays]


def position():
    return lax.axis_index("comp").astype(jnp.int32), lax.axis_index("trc").astype(jnp.int32)


def roll(x, shift, axis):
    return pltpu.roll(x, shift % x.shape[axis], axis)


def pack_kernel(field, u, v, k, h, m, *refs):
    segments, (low, high), (west, east, mask, sem) = refs[:4], refs[4:6], refs[6:]
    levels, width = field.shape[0], field.shape[1]
    depth = u.shape[0]
    comps = len(segments)
    group = levels // comps
    copies = []

    def copy(src, dst):
        copies.append(pltpu.make_async_copy(src, dst, sem.at[len(copies)]))
        copies[-1].start()

    place, _ = position()
    for index, source in enumerate((u, v, k)):
        rows = pl.ds(index * depth, depth)
        copy(source.at[:, width - 8 :, :], low.at[rows])
        copy(source.at[:, :8, :], high.at[rows])
    copy(h.at[width - 8 :, :], low.at[3 * depth])
    copy(h.at[:8, :], high.at[3 * depth])
    copy(m.at[width - 8 :, :], mask.at[0])
    copy(m.at[:8, :], mask.at[1])
    copy(field.at[:, :8, :], west)
    copy(field.at[:, width - 8 :, :], east)
    for shift, segment in enumerate(segments):
        target = lax.rem(place + shift, comps)
        start = group * target
        copy(field.at[pl.ds(start, group)], segment.at[pl.ds(HALO, group)])
        copy(field.at[pl.ds(jnp.maximum(start - HALO, 0), HALO)], segment.at[pl.ds(0, HALO)])
        after = jnp.minimum(start + group, levels - HALO)
        copy(field.at[pl.ds(after, HALO)], segment.at[pl.ds(HALO + group, HALO)])
    for item in copies[:12]:
        item.wait()
    low[3 * depth + 1] = mask[0].astype(jnp.float32)
    high[3 * depth + 1] = mask[1].astype(jnp.float32)
    half = levels // 2
    first = 3 * depth + 2
    upper = lax.broadcasted_iota(jnp.int32, west.shape[1:], 0) < HALO

    def body(level, carry):
        a, b = west[level], west[level + half]
        high[first + level] = jnp.where(upper, a, roll(b, HALO, 0))
        a, b = east[level], east[level + half]
        low[first + level] = jnp.where(upper, roll(b, HALO, 0), a)
        return carry

    lax.fori_loop(0, half, body, 0, unroll=4)
    for item in copies[12:]:
        item.wait()


def side_kernel(first, low, high, inner, *refs):
    segments, side = refs[:4], refs[4]
    width = inner.shape[1]
    levels = side.shape[0]
    half = levels // 2
    comps = len(segments)
    group = levels // comps
    c, _ = position()
    upper = lax.broadcasted_iota(jnp.int32, side.shape[1:], 0) < HALO

    def body(level, carry):
        a, b = high[first + level], low[first + level]
        side[level] = jnp.where(upper, a, b)
        side[level + half] = roll(jnp.where(upper, b, a), HALO, 0)
        return carry

    lax.fori_loop(0, half, body, 0, unroll=4)
    for shift, segment in enumerate(segments):
        start = group * lax.rem(c + shift, comps)
        if shift == SHIFTS[-1]:
            segment[:, :width, :] = inner[...]
            segment = segment.at[:, width:, :]
        segment[pl.ds(HALO, group)] = side[pl.ds(start, group)]
        segment[pl.ds(0, HALO)] = side[pl.ds(jnp.maximum(start - HALO, 0), HALO)]
        segment[pl.ds(HALO + group, HALO)] = side[pl.ds(jnp.minimum(start + group, levels - HALO), HALO)]


def ocean_kernel(last, u_ref, v_ref, k_ref, h_ref, m_ref, lo_ref, hi_ref, east_ref, north_ref, flux_ref):
    depth, width, rows = u_ref.shape

    def circular(inner, index):
        return jnp.concatenate([inner, hi_ref[index], lo_ref[index]], 0)

    c, t = position()
    first_level = (c * lax.axis_size("trc") + t) * depth
    span = width + 16
    lane = lax.broadcasted_iota(jnp.int32, (span, rows), 1)
    first, final = lane == 0, lane == rows - 1
    east = lambda x: roll(x, -1, 0)
    west = lambda x: roll(x, 1, 0)
    north = lambda x: jnp.where(final, 0.0, roll(x, -1, 1))
    south = lambda x: jnp.where(first, 0.0, roll(x, 1, 1))
    coriolis = 0.5 + 0.5 * lane.astype(jnp.float32) / rows
    h = circular(h_ref[...], 3 * depth)
    wet = circular(m_ref[...].astype(jnp.float32), 3 * depth + 1)
    slope_x = east(h) - h
    slope_y = north(h) - h
    open_x = wet * east(wet)
    open_y = wet * north(wet)
    upper = lax.broadcasted_iota(jnp.int32, (8, rows), 0) < HALO

    def emit(index, level, x):
        flux_ref[index, level, :width, :] = x[:width]
        flux_ref[index, level, width:, :] = jnp.where(upper, x[width : width + 8], x[width + 8 :])

    for level in range(depth):
        u = circular(u_ref[level], level)
        v = circular(v_ref[level], depth + level)
        mixing = circular(k_ref[level], 2 * depth + level)
        lap = east(u) + west(u) + north(u) + south(u) - 4.0 * u
        pair = v + east(v)
        avg = 0.25 * (pair + south(pair))
        east_new = open_x * (u + TIME_STEP * (coriolis * avg - slope_x + VISCOSITY * lap))
        lap = east(v) + west(v) + north(v) + south(v) - 4.0 * v
        pair = u + west(u)
        avg = 0.25 * (pair + north(pair))
        north_new = open_y * (v + TIME_STEP * (-coriolis * avg - slope_y + VISCOSITY * lap))
        speed = jnp.minimum(east_new * east_new + north_new * north_new, 1.0)
        keep = jnp.where(first_level + level < last, 1.0, 0.0)
        kappa = wet * mixing * (1.0 + speed) * keep
        east_ref[level] = east_new[:width]
        north_ref[level] = north_new[:width]
        emit(0, level, COURANT * east_new)
        emit(1, level, COURANT * north_new)
        emit(2, level, kappa)


def weight_kernel(own, core, pair, core_pair, weight_ref):
    depth = own.shape[1]
    _, t = position()
    odd = t & 1

    def fill(position, piece):
        for level in range(depth):
            fx, fy, kappa = piece(0, level), piece(1, level), piece(2, level)
            fw, fs = roll(fx, 1, 0), roll(fy, 1, 1)
            index = position * depth + level
            weight_ref[0, index] = (
                1.0
                - (jnp.maximum(fx, 0.0) - jnp.minimum(fw, 0.0))
                - (jnp.maximum(fy, 0.0) - jnp.minimum(fs, 0.0))
            )
            weight_ref[1, index] = -jnp.minimum(fx, 0.0)
            weight_ref[2, index] = jnp.maximum(fw, 0.0)
            weight_ref[3, index] = -jnp.minimum(fy, 0.0)
            weight_ref[4, index] = jnp.maximum(fs, 0.0)
            weight_ref[5, index] = kappa

    fill(1 + t, lambda i, l: own[i, l])
    fill(1 + (t ^ 1), lambda i, l: core[i, l])
    fill(1 + (t ^ 2), lambda i, l: pair[0, i, l])
    fill(1 + (t ^ 3), lambda i, l: core_pair[0, i, l])
    fill(5 * odd, lambda i, l: pair[1, i, l])
    fill(5 * (1 - odd), lambda i, l: core_pair[1, i, l])


def pair_kernel(across, near, far, out):
    out[0] = across[...]
    out[1] = near[...] + far[...]


def transport_kernel(levels, weight, *refs):
    parts, (mine_ref, other_ref, send_ref, sums_ref, a, b) = refs[:-6], refs[-6:]
    total, _, _ = parts[0].shape
    width = mine_ref.shape[1]
    _, t = position()
    if len(parts) == 2:
        inner, side = parts

        def fill(level, carry):
            a[level, :width, :] = inner[level]
            a[level, width:, :] = side[level]
            return carry

        lax.fori_loop(0, total, fill, 0, unroll=4)
        whole = a
    else:
        whole = parts[0]

    def edge(src, level):
        return weight[5, level] * (src[level + 1] - src[level])

    def update(src, level, above):
        c = src[level]
        below = weight[5, level] * (src[level + 1] - c)
        value = (
            weight[0, level] * c
            + weight[1, level] * roll(c, -1, 0)
            + weight[2, level] * roll(c, 1, 0)
            + weight[3, level] * roll(c, -1, 1)
            + weight[4, level] * roll(c, 1, 1)
            + (below - above)
        )
        return value, below

    for step in range(SUBSTEPS - 1):
        src, dst = (b, a) if step % 2 else (whole if step == 0 else a, b)
        start, stop = step + 1, total - 1 - step

        def body(index, above, src=src, dst=dst, start=start):
            for sub in range(4):
                level = start + 4 * index + sub
                dst[level], above = update(src, level, above)
            return above

        trips = (stop - start) // 4
        above = lax.fori_loop(0, trips, body, edge(src, start - 1))
        for level in range(start + 4 * trips, stop):
            dst[level], above = update(src, level, above)
    src = b if SUBSTEPS % 2 == 0 else a
    outs = (mine_ref, other_ref, send_ref, send_ref)
    for place, out in enumerate(outs):
        block = t ^ place
        first = HALO + HALO * block
        above = edge(src, first - 1)
        tau = None
        for sub in range(HALO):
            value, above = update(src, first + sub, above)
            m = value[:width]
            out[sub + (HALO if place == 3 else 0)] = m
            part = (0.5 + m * m) / levels
            tau = part if tau is None else tau + part
        sums_ref[block] = tau


def tau_kernel(holder, sums, *refs):
    out = refs[-1]
    c, t = position()
    total = sums[0]
    for index in range(1, sums.shape[0]):
        total = total + sums[index]
    for above in refs[:-1]:
        total = total + above[...]
    out[...] = jnp.where((t == 0) & (c == holder), total, 0.0)


def start_kernel(*refs):
    bases, sums, near, far = refs[:3], refs[3:7], refs[7], refs[8]
    c, _ = position()
    turn = functools.reduce(lambda x, i: jnp.where(c == SHIFTS[i], i, x), range(4), 0)
    running = bases[0][...] + bases[1][...] + bases[2][...]
    for index in range(4):
        out = near if index < 2 else far
        out[index % 2] = running
        for i in range(4):
            running = running + jnp.where(turn == i, sums[i][index], 0.0)


def gather_kernel(near, far, *refs):
    others, across, out = refs[:4], refs[4:8], refs[8]
    depth = others[0].shape[0]
    _, t = position()
    for slot in range(4):
        out[slot * depth : (slot + 1) * depth] = others[slot][...]
        out[(4 + slot) * depth : (5 + slot) * depth] = across[slot][depth:]
    out[8 * depth] = jnp.where(t == 0, near[1], far[1])


def reaction_kernel(levels, react_ref, sun_ref, near_ref, far_ref, *refs):
    mine = refs[0:4]
    across = refs[4:8]
    core_ref, out_ref, heat_ref, depth, field = refs[8:]
    rows = out_ref.shape[2]
    count = out_ref.shape[0]
    level = pl.program_id(0)
    deep = pl.num_programs(0)
    c, t = position()

    @pl.when(level == 0)
    def _():
        inner = jnp.where(t == 0, near_ref[0], far_ref[0])
        depth[...] = jnp.where(t % 2 == 0, inner, core_ref[8 * deep])

    trcs = lax.axis_size("trc")
    comps = lax.axis_size("comp")
    for slot, shift in enumerate(SHIFTS):
        first = trcs * lax.rem(c + comps - shift, comps)
        field[first + t] = mine[slot][level]
        field[first + (t ^ 2)] = across[slot][level]
        field[first + (t ^ 1)] = core_ref[slot * deep + level]
        field[first + (t ^ 3)] = core_ref[(4 + slot) * deep + level]

    def chunk(index, carry):
        row = pl.ds(pl.multiple_of(index * 8, 8), 8)
        m = [field[j, row, :] for j in range(count)]
        tau = (0.5 + m[0] * m[0]) / levels
        above = depth[row, :]
        light_top = sun_ref[row, :] * jnp.exp(-above)
        heat_ref[0, row, :] = levels * light_top * (1.0 - jnp.exp(-tau))
        depth[row, :] = above + tau
        light_mid = light_top * jnp.exp(-0.5 * tau)
        limit = light_mid / (light_mid + HALF_LIGHT)
        for i in range(count):
            growth = react_ref[i, 0] * m[0]
            for j in range(1, count):
                growth = growth + react_ref[i, j] * m[j]
            out_ref[i, 0, row, :] = m[i] + limit * growth
        return carry

    lax.fori_loop(0, rows // 8, chunk, 0)


def per_device(tracers, eastward, northward, surface_height, sea_mask, mixing, sunlight, reaction):
    i32 = jnp.int32
    depth, width, rows = eastward.shape
    comps, trcs = lax.axis_size("comp"), lax.axis_size("trc")
    tiles = lax.axis_size("horiz")
    levels = depth * comps * trcs
    group = depth * trcs
    tall = group + 2 * HALO
    span = width + 2 * HALO
    forward = [(i, i + 1) for i in range(tiles - 1)]
    backward = [(i + 1, i) for i in range(tiles - 1)]
    flip_x = [(i, i ^ 2) for i in range(trcs)]
    flip_core = [(i, i ^ 1) for i in range(trcs)]
    both = ("comp", "trc")
    edges = 3 * depth + 2
    payload = edges + levels // 2

    def ring(shift):
        return [(i, (i + shift) % comps) for i in range(comps)]

    packed = call(
        pack_kernel,
        4,
        out_shape=(local(tall, width, rows),) * comps + (local(payload, 8, rows),) * 2,
        in_specs=[ANY] * 6,
        out_specs=(VMEM,) * (comps + 2),
        scratch_shapes=[
            local(levels, 8, rows),
            local(levels, 8, rows),
            pltpu.VMEM((2, 8, rows), i32),
            pltpu.SemaphoreType.DMA((12 + 3 * comps,)),
        ],
    )(*in_hbm(tracers[0], eastward, northward, mixing, surface_height, sea_mask))
    inner = list(packed[:comps])
    low = lax.ppermute(packed[comps], "horiz", forward)
    high = lax.ppermute(packed[comps + 1], "horiz", backward)
    inner[1] = lax.ppermute(inner[1], "comp", ring(1))
    inner[3] = lax.ppermute(inner[3], "comp", ring(3))

    east_out, north_out, flux = call(
        functools.partial(ocean_kernel, levels - 1),
        4,
        out_shape=(array(depth, width, rows),) * 2 + (local(3, depth, span, rows),),
        in_specs=[VMEM] * 7,
        out_specs=(VMEM,) * 3,
    )(eastward, northward, mixing, surface_height, sea_mask, low, high)

    ups = range(comps - 1)
    last, nxt = trcs - 1, trcs
    near = lax.ppermute(
        flux,
        both,
        [(trcs * i + last, trcs * i + nxt + 2) for i in ups] + [(trcs * i + nxt, trcs * i + 1) for i in ups],
    )
    far = lax.ppermute(
        flux,
        both,
        [(trcs * i + last, trcs * i + nxt) for i in ups] + [(trcs * i + nxt, trcs * i + last) for i in ups],
    )
    across_flux = lax.ppermute(flux, "trc", flip_x)
    core_flux = lax.ppermute(flux, "trc", flip_core)

    sides = list(
        call(
            functools.partial(side_kernel, edges),
            1,
            out_shape=tuple(local(tall, span if i == SHIFTS[-1] else 8, rows) for i in range(comps)),
            in_specs=[VMEM] * 3,
            out_specs=(VMEM,) * comps,
            scratch_shapes=[local(levels, 8, rows)],
        )(*in_vmem(low, high, inner[2]))
    )
    for shift in (1, 3, 2):
        sides[shift] = lax.ppermute(sides[shift], "comp", ring(shift))
    pair = call(
        pair_kernel,
        1,
        out_shape=local(2, 3, depth, span, rows),
        in_specs=[VMEM] * 3,
        out_specs=VMEM,
    )(across_flux, near, far)
    core_pair = lax.ppermute(pair, "trc", flip_core)
    weight = call(
        weight_kernel, 3, out_shape=local(6, tall, span, rows), in_specs=[VMEM] * 4, out_specs=VMEM
    )(*in_vmem(flux, core_flux, pair, core_pair))
    piece = local(depth, width, rows)
    mine, other, across, sums = [], [], [], []
    bases = []

    def pass_tau(turn, holder):
        value = call(
            functools.partial(tau_kernel, holder),
            1,
            out_shape=local(width, rows),
            in_specs=[VMEM] * (1 + len(bases[-1:])),
            out_specs=VMEM,
        )(*in_vmem(sums[turn], *bases[-1:]))
        bases.append(lax.ppermute(value, "comp", [(holder, holder + 1)]))

    for turn, shift in enumerate(SHIFTS):
        inputs = [weight] + ([inner[shift]] if turn < 3 else []) + [sides[shift]]
        m, o, s, total = call(
            functools.partial(transport_kernel, levels),
            6,
            out_shape=(piece, piece, local(2 * depth, width, rows), piece),
            in_specs=[VMEM] * len(inputs),
            out_specs=(VMEM,) * 4,
            scratch_shapes=[local(tall, span, rows)] * 2,
        )(*in_vmem(*inputs))
        mine.append(m)
        other.append(o)
        across.append(lax.ppermute(s, "trc", flip_x))
        sums.append(total)
        if shift < comps - 1:
            pass_tau(turn, shift)
    near, far = call(
        start_kernel,
        1,
        out_shape=(local(2, width, rows),) * 2,
        in_specs=[VMEM] * 7,
        out_specs=(VMEM,) * 2,
    )(*in_vmem(*bases, *sums))
    far = lax.ppermute(far, "trc", flip_x)
    cross = call(
        gather_kernel,
        2,
        out_shape=local(8 * depth + 1, width, rows),
        in_specs=[VMEM] * 10,
        out_specs=VMEM,
    )(*in_vmem(near, far, *other, *across))
    cross = lax.ppermute(cross, "trc", flip_core)

    count = reaction.shape[0]
    tracers_out, heating = call(
        functools.partial(reaction_kernel, levels),
        6,
        grid=(depth,),
        out_shape=(array(count, depth, width, rows), array(depth, width, rows)),
        in_specs=[SMEM] + [VMEM] * 12,
        out_specs=(
            pl.BlockSpec((count, 1, width, rows), lambda l: (0, l, 0, 0)),
            pl.BlockSpec((1, width, rows), lambda l: (l, 0, 0)),
        ),
        scratch_shapes=[local(width, rows), local(count, width, rows)],
    )(reaction, *in_vmem(sunlight, near, far, *mine, *across, cross))
    return (east_out, north_out, tracers_out, heating)


def solution(mesh):
    return jax.shard_map(
        per_device,
        mesh=mesh,
        in_specs=(
            P(("comp", "trc"), None, "horiz", None),
            P(("comp", "trc"), "horiz", None),
            P(("comp", "trc"), "horiz", None),
            P("horiz", None),
            P("horiz", None),
            P(("comp", "trc"), "horiz", None),
            P("horiz", None),
            P(),
        ),
        out_specs=(
            P(("comp", "trc"), "horiz", None),
            P(("comp", "trc"), "horiz", None),
            P(None, ("comp", "trc"), "horiz", None),
            P(("comp", "trc"), "horiz", None),
        ),
        check_vma=False,
    )
```

```python
import functools

import jax
import jax.numpy as jnp
from jax import lax
from jax.experimental import pallas as pl
from jax.experimental.pallas import tpu as pltpu
from jax.sharding import PartitionSpec as P


SUBSTEPS = 4
TIME_STEP = 0.25
VISCOSITY = 0.05
COURANT = 0.2
HALF_LIGHT = 0.3

HALO = 4


SMEM = pl.BlockSpec(memory_space=pltpu.SMEM)
VMEM = pl.BlockSpec(memory_space=pltpu.VMEM)
ANY = pl.BlockSpec(memory_space=pl.ANY)


def local(*shape):
    return pltpu.VMEM(shape, jnp.float32)


def array(*shape):
    return jax.ShapeDtypeStruct(shape, jnp.float32)


def call(kernel, cost, **kwargs):
    return pl.pallas_call(
        kernel,
        compiler_params=pltpu.CompilerParams(vmem_limit_bytes=12 << 20),
        cost_estimate=pl.CostEstimate(flops=cost * 1_000_000, bytes_accessed=cost * 1_000_000, transcendentals=0),
        **kwargs,
    )


def in_hbm(*arrays):
    return [pltpu.with_memory_space_constraint(x, pltpu.HBM) for x in arrays]


def in_vmem(*arrays):
    return [pltpu.with_memory_space_constraint(x, pltpu.VMEM) for x in arrays]


def position():
    return lax.axis_index("comp").astype(jnp.int32), lax.axis_index("trc").astype(jnp.int32)


def shift_of(turn, t):
    if turn < 2:
        return turn
    return jnp.where(t == 0, turn, 5 - turn)


def roll(x, shift, axis):
    return pltpu.roll(x, shift % x.shape[axis], axis)


def segment_copies(field, segment, shift):
    levels = field.shape[0]
    group = segment.shape[0] - 2 * HALO
    comps = levels // group
    c, _ = position()
    start = group * lax.rem(c + shift, comps)
    after = jnp.minimum(start + group, levels - HALO)
    return [
        (field.at[pl.ds(start, group)], segment.at[pl.ds(HALO, group)]),
        (field.at[pl.ds(jnp.maximum(start - HALO, 0), HALO)], segment.at[pl.ds(0, HALO)]),
        (field.at[pl.ds(after, HALO)], segment.at[pl.ds(HALO + group, HALO)]),
    ]


def pack_kernel(field, u, v, k, h, m, one, three, low, high, side_low, side_high, west, east, mask, sem):
    levels, width = field.shape[0], field.shape[1]
    depth = u.shape[0]
    copies = []

    def copy(src, dst):
        copies.append(pltpu.make_async_copy(src, dst, sem.at[len(copies)]))
        copies[-1].start()

    for index, source in enumerate((u, v, k)):
        rows = pl.ds(index * depth, depth)
        copy(source.at[:, width - 8 :, :], low.at[rows])
        copy(source.at[:, :8, :], high.at[rows])
    copy(h.at[width - 8 :, :], low.at[3 * depth])
    copy(h.at[:8, :], high.at[3 * depth])
    copy(m.at[width - 8 :, :], mask.at[0])
    copy(m.at[:8, :], mask.at[1])
    copy(field.at[:, :8, :], west)
    copy(field.at[:, width - 8 :, :], east)
    _, t = position()
    for shift, segment in ((1, one), (shift_of(2, t), three)):
        for src, dst in segment_copies(field, segment, shift):
            copy(src, dst)
    for item in copies[:12]:
        item.wait()
    low[3 * depth + 1] = mask[0].astype(jnp.float32)
    high[3 * depth + 1] = mask[1].astype(jnp.float32)
    half = levels // 2
    upper = lax.broadcasted_iota(jnp.int32, west.shape[1:], 0) < HALO

    def body(level, carry):
        a, b = west[level], west[level + half]
        side_high[level] = jnp.where(upper, a, roll(b, HALO, 0))
        a, b = east[level], east[level + half]
        side_low[level] = jnp.where(upper, roll(b, HALO, 0), a)
        return carry

    lax.fori_loop(0, half, body, 0, unroll=4)
    for item in copies[12:]:
        item.wait()


def side_kernel(field, low, high, own, one, two, three, side, sem):
    levels = side.shape[0]
    half = levels // 2
    width = field.shape[1]
    comps = lax.axis_size("comp")
    group = levels // comps
    c, t = position()
    upper = lax.broadcasted_iota(jnp.int32, side.shape[1:], 0) < HALO
    copies = []
    for shift, segment in ((0, own), (shift_of(3, t), two)):
        for src, dst in segment_copies(field, segment.at[:, :width, :], shift):
            copies.append(pltpu.make_async_copy(src, dst, sem.at[len(copies)]))
            copies[-1].start()

    def body(level, carry):
        a, b = high[level], low[level]
        side[level] = jnp.where(upper, a, b)
        side[level + half] = roll(jnp.where(upper, b, a), HALO, 0)
        return carry

    lax.fori_loop(0, half, body, 0, unroll=4)
    for turn, segment in enumerate((own, one, three, two)):
        start = group * lax.rem(c + shift_of(turn, t), comps)
        columns = slice(width if turn in (0, 3) else 0, None)
        segment[pl.ds(HALO, group), columns, :] = side[pl.ds(start, group)]
        segment[pl.ds(0, HALO), columns, :] = side[pl.ds(jnp.maximum(start - HALO, 0), HALO)]
        segment[pl.ds(HALO + group, HALO), columns, :] = side[pl.ds(jnp.minimum(start + group, levels - HALO), HALO)]
    for item in copies:
        item.wait()


def ocean_kernel(last, u_ref, v_ref, k_ref, h_ref, m_ref, lo_ref, hi_ref, east_ref, north_ref, flux_ref):
    depth, width, rows = u_ref.shape

    def circular(inner, index):
        return jnp.concatenate([inner, hi_ref[index], lo_ref[index]], 0)

    c, t = position()
    first_level = (c * lax.axis_size("trc") + t) * depth
    span = width + 16
    lane = lax.broadcasted_iota(jnp.int32, (span, rows), 1)
    first, final = lane == 0, lane == rows - 1
    east = lambda x: roll(x, -1, 0)
    west = lambda x: roll(x, 1, 0)
    north = lambda x: jnp.where(final, 0.0, roll(x, -1, 1))
    south = lambda x: jnp.where(first, 0.0, roll(x, 1, 1))
    coriolis = 0.5 + 0.5 * lane.astype(jnp.float32) / rows
    h = circular(h_ref[...], 3 * depth)
    wet = circular(m_ref[...].astype(jnp.float32), 3 * depth + 1)
    slope_x = east(h) - h
    slope_y = north(h) - h
    open_x = wet * east(wet)
    open_y = wet * north(wet)
    upper = lax.broadcasted_iota(jnp.int32, (8, rows), 0) < HALO

    def emit(index, level, x):
        flux_ref[index, level, :width, :] = x[:width]
        flux_ref[index, level, width:, :] = jnp.where(upper, x[width : width + 8], x[width + 8 :])

    for level in range(depth):
        u = circular(u_ref[level], level)
        v = circular(v_ref[level], depth + level)
        mixing = circular(k_ref[level], 2 * depth + level)
        lap = east(u) + west(u) + north(u) + south(u) - 4.0 * u
        pair = v + east(v)
        avg = 0.25 * (pair + south(pair))
        east_new = open_x * (u + TIME_STEP * (coriolis * avg - slope_x + VISCOSITY * lap))
        lap = east(v) + west(v) + north(v) + south(v) - 4.0 * v
        pair = u + west(u)
        avg = 0.25 * (pair + north(pair))
        north_new = open_y * (v + TIME_STEP * (-coriolis * avg - slope_y + VISCOSITY * lap))
        speed = jnp.minimum(east_new * east_new + north_new * north_new, 1.0)
        keep = jnp.where(first_level + level < last, 1.0, 0.0)
        kappa = wet * mixing * (1.0 + speed) * keep
        east_ref[level] = east_new[:width]
        north_ref[level] = north_new[:width]
        emit(0, level, COURANT * east_new)
        emit(1, level, COURANT * north_new)
        emit(2, level, kappa)


def weight_kernel(own, core, pair, core_pair, weight_ref):
    depth = own.shape[1]
    _, t = position()
    odd = t & 1

    def fill(position, piece):
        for level in range(depth):
            fx, fy, kappa = piece(0, level), piece(1, level), piece(2, level)
            fw, fs = roll(fx, 1, 0), roll(fy, 1, 1)
            index = position * depth + level
            weight_ref[0, index] = (
                1.0
                - (jnp.maximum(fx, 0.0) - jnp.minimum(fw, 0.0))
                - (jnp.maximum(fy, 0.0) - jnp.minimum(fs, 0.0))
            )
            weight_ref[1, index] = -jnp.minimum(fx, 0.0)
            weight_ref[2, index] = jnp.maximum(fw, 0.0)
            weight_ref[3, index] = -jnp.minimum(fy, 0.0)
            weight_ref[4, index] = jnp.maximum(fs, 0.0)
            weight_ref[5, index] = kappa

    fill(1 + t, lambda i, l: own[i, l])
    fill(1 + (t ^ 1), lambda i, l: core[i, l])
    fill(1 + (t ^ 2), lambda i, l: pair[0, i, l])
    fill(1 + (t ^ 3), lambda i, l: core_pair[0, i, l])
    fill(5 * odd, lambda i, l: pair[1, i, l])
    fill(5 * (1 - odd), lambda i, l: core_pair[1, i, l])


def pair_kernel(across, near, far, out):
    out[0] = across[...]
    out[1] = near[...] + far[...]


def transport_kernel(levels, turn, weight, *refs):
    parts, refs = refs[: 2 - (turn in (0, 3))], refs[2 - (turn in (0, 3)) :]
    if turn == 3:
        earlier, near_ref, refs = refs[:3], refs[3], refs[4:]
    mine_ref, other_ref, send_ref, sums_ref, a, b = refs
    total, _, _ = parts[0].shape
    width = mine_ref.shape[1]
    c, t = position()
    if len(parts) == 2:
        inner, side = parts

        def fill(level, carry):
            a[level, :width, :] = inner[level]
            a[level, width:, :] = side[level]
            return carry

        lax.fori_loop(0, total, fill, 0, unroll=4)
        whole = a
    else:
        whole = parts[0]

    def edge(src, level):
        return weight[5, level] * (src[level + 1] - src[level])

    def update(src, level, above):
        c = src[level]
        below = weight[5, level] * (src[level + 1] - c)
        value = (
            weight[0, level] * c
            + weight[1, level] * roll(c, -1, 0)
            + weight[2, level] * roll(c, 1, 0)
            + weight[3, level] * roll(c, -1, 1)
            + weight[4, level] * roll(c, 1, 1)
            + (below - above)
        )
        return value, below

    for step in range(SUBSTEPS - 1):
        src, dst = (b, a) if step % 2 else (whole if step == 0 else a, b)
        start, stop = step + 1, total - 1 - step

        def body(index, above, src=src, dst=dst, start=start):
            for sub in range(4):
                level = start + 4 * index + sub
                dst[level], above = update(src, level, above)
            return above

        trips = (stop - start) // 4
        above = lax.fori_loop(0, trips, body, edge(src, start - 1))
        for level in range(start + 4 * trips, stop):
            dst[level], above = update(src, level, above)
    src = b if SUBSTEPS % 2 == 0 else a
    outs = (mine_ref, other_ref, send_ref, send_ref)
    for place, out in enumerate(outs):
        block = t ^ place
        first = HALO + HALO * block
        above = edge(src, first - 1)
        tau = None
        for sub in range(HALO):
            value, above = update(src, first + sub, above)
            m = value[:width]
            out[sub + (HALO if place == 3 else 0)] = m
            part = (0.5 + m * m) / levels
            tau = part if tau is None else tau + part
        sums_ref[block] = tau
    zero = jnp.zeros(sums_ref.shape[1:], jnp.float32)

    def thickness(index, *by_comp):
        total = zero
        for holder, part in by_comp:
            total = total + jnp.where((t == 0) & (c == holder), part[index], 0.0)
        return total

    if turn < 3:
        send_ref[2 * HALO] = sum((thickness(index, (turn, sums_ref)) for index in range(4)), zero)
    else:
        running = zero
        for index in range(4):
            if index < 2:
                near_ref[index] = running
            else:
                send_ref[2 * HALO + index - 2] = running
            running = running + thickness(index, *enumerate((*earlier, sums_ref)))


def tau_kernel(*refs):
    sent, received, whole = refs[: len(refs) // 2], refs[len(refs) // 2 : -1], refs[-1]
    _, t = position()
    total = jnp.zeros(whole.shape, jnp.float32)
    for here, there in zip(sent, received):
        total = total + jnp.where(t == 0, here[2 * HALO], jnp.where(t == 2, there[2 * HALO], 0.0))
    whole[...] = total


def gather_kernel(near, one, two, three, *refs):
    others, across, out = refs[:4], refs[4:8], refs[8]
    depth = others[0].shape[0]
    _, t = position()
    for turn in range(4):
        out[turn * depth : (turn + 1) * depth] = others[turn][...]
        out[(4 + turn) * depth : (5 + turn) * depth] = across[turn][depth : 2 * depth]
    base = one[...] + two[...] + three[...]
    out[8 * depth] = base + jnp.where(t == 0, near[1], across[3][2 * depth + 1])


def reaction_kernel(levels, react_ref, sun_ref, near_ref, one, two, three, *refs):
    mine = refs[0:4]
    across = refs[4:8]
    core_ref, out_ref, heat_ref, depth, field = refs[8:]
    rows = out_ref.shape[2]
    count = out_ref.shape[0]
    level = pl.program_id(0)
    deep = pl.num_programs(0)
    c, t = position()

    @pl.when(level == 0)
    def _():
        base = one[...] + two[...] + three[...]
        inner = base + jnp.where(t == 0, near_ref[0], across[3][2 * HALO])
        depth[...] = jnp.where(t % 2 == 0, inner, core_ref[8 * deep])

    trcs = lax.axis_size("trc")
    comps = lax.axis_size("comp")
    for turn in range(4):

        def tracer(holder, turn=turn):
            return trcs * lax.rem(c + comps - shift_of(turn, holder), comps) + holder

        field[tracer(t)] = mine[turn][level]
        field[tracer(t ^ 2)] = across[turn][level]
        field[tracer(t ^ 1)] = core_ref[turn * deep + level]
        field[tracer(t ^ 3)] = core_ref[(4 + turn) * deep + level]

    def chunk(index, carry):
        row = pl.ds(pl.multiple_of(index * 8, 8), 8)
        m = [field[j, row, :] for j in range(count)]
        tau = (0.5 + m[0] * m[0]) / levels
        above = depth[row, :]
        light_top = sun_ref[row, :] * jnp.exp(-above)
        heat_ref[0, row, :] = levels * light_top * (1.0 - jnp.exp(-tau))
        depth[row, :] = above + tau
        light_mid = light_top * jnp.exp(-0.5 * tau)
        limit = light_mid / (light_mid + HALF_LIGHT)
        for i in range(count):
            growth = react_ref[i, 0] * m[0]
            for j in range(1, count):
                growth = growth + react_ref[i, j] * m[j]
            out_ref[i, 0, row, :] = m[i] + limit * growth
        return carry

    lax.fori_loop(0, rows // 8, chunk, 0)


def per_device(tracers, eastward, northward, surface_height, sea_mask, mixing, sunlight, reaction):
    i32 = jnp.int32
    depth, width, rows = eastward.shape
    comps, trcs = lax.axis_size("comp"), lax.axis_size("trc")
    tiles = lax.axis_size("horiz")
    levels = depth * comps * trcs
    group = depth * trcs
    tall = group + 2 * HALO
    span = width + 2 * HALO
    forward = [(i, i + 1) for i in range(tiles - 1)]
    backward = [(i + 1, i) for i in range(tiles - 1)]
    flip_x = [(i, i ^ 2) for i in range(trcs)]
    flip_core = [(i, i ^ 1) for i in range(trcs)]
    both = ("comp", "trc")
    edges = 3 * depth + 2

    def ring(*shifts):
        return [
            (trcs * i + j, trcs * ((i + shifts[min(j, len(shifts) - 1)]) % comps) + j)
            for i in range(comps)
            for j in range(trcs)
        ]

    packed = call(
        pack_kernel,
        4,
        out_shape=(local(tall, width, rows),) * 2
        + (local(edges, 8, rows),) * 2
        + (local(levels // 2, 8, rows),) * 2,
        in_specs=[ANY] * 6,
        out_specs=(VMEM,) * 6,
        scratch_shapes=[
            local(levels, 8, rows),
            local(levels, 8, rows),
            pltpu.VMEM((2, 8, rows), i32),
            pltpu.SemaphoreType.DMA((18,)),
        ],
    )(*in_hbm(tracers[0], eastward, northward, mixing, surface_height, sea_mask))
    one, three, low, high, side_low, side_high = packed
    one = lax.ppermute(one, both, ring(1))
    three = lax.ppermute(three, both, ring(2, 3))
    low = lax.ppermute(low, "horiz", forward)
    high = lax.ppermute(high, "horiz", backward)
    side_low = lax.ppermute(side_low, "horiz", forward)
    side_high = lax.ppermute(side_high, "horiz", backward)

    east_out, north_out, flux = call(
        functools.partial(ocean_kernel, levels - 1),
        4,
        out_shape=(array(depth, width, rows),) * 2 + (local(3, depth, span, rows),),
        in_specs=[VMEM] * 7,
        out_specs=(VMEM,) * 3,
    )(eastward, northward, mixing, surface_height, sea_mask, low, high)

    ups = range(comps - 1)
    last, nxt = trcs - 1, trcs
    near = lax.ppermute(
        flux,
        both,
        [(trcs * i + last, trcs * i + nxt + 2) for i in ups] + [(trcs * i + nxt, trcs * i + 1) for i in ups],
    )
    far = lax.ppermute(near, "trc", [(trcs - 2, 0), (1, trcs - 1)])
    across_flux = lax.ppermute(flux, "trc", flip_x)
    core_flux = lax.ppermute(flux, "trc", flip_core)

    whole = local(tall, span, rows)
    flank = local(tall, 8, rows)
    own, side_one, two, side_three = call(
        side_kernel,
        1,
        out_shape=(whole, flank, whole, flank),
        in_specs=[ANY, VMEM, VMEM],
        out_specs=(VMEM,) * 4,
        scratch_shapes=[local(levels, 8, rows), pltpu.SemaphoreType.DMA((6,))],
    )(*in_hbm(tracers[0]), *in_vmem(side_low, side_high))
    side_one = lax.ppermute(side_one, both, ring(1))
    side_three = lax.ppermute(side_three, both, ring(2, 3))
    two = lax.ppermute(two, both, ring(3, 2))
    parts = ((own,), (one, side_one), (three, side_three), (two,))
    pair = call(
        pair_kernel,
        1,
        out_shape=local(2, 3, depth, span, rows),
        in_specs=[VMEM] * 3,
        out_specs=VMEM,
    )(across_flux, near, far)
    core_pair = lax.ppermute(pair, "trc", flip_core)
    weight = call(
        weight_kernel, 3, out_shape=local(6, tall, span, rows), in_specs=[VMEM] * 4, out_specs=VMEM
    )(*in_vmem(flux, core_flux, pair, core_pair))
    piece = local(depth, width, rows)
    mine, other, sends, across, sums = [], [], [], [], []
    for turn in range(4):
        inputs = [weight, *parts[turn]]
        sent = 2 * depth
        if turn == 3:
            inputs += sums
        sent += 2 if turn == 3 else 1
        results = call(
            functools.partial(transport_kernel, levels, turn),
            6,
            out_shape=(local(2, width, rows),) * (turn == 3)
            + (piece, piece, local(sent, width, rows), piece),
            in_specs=[VMEM] * len(inputs),
            out_specs=(VMEM,) * (5 if turn == 3 else 4),
            scratch_shapes=[local(tall, span, rows)] * 2,
        )(*in_vmem(*inputs))
        m, o, held, total = results[-4:]
        mine.append(m)
        other.append(o)
        sends.append(held)
        across.append(lax.ppermute(held, "trc", flip_x))
        sums.append(total)
    near = results[0]
    bases = []
    for k in range(1, comps):
        known = comps - k
        thick = call(
            tau_kernel,
            1,
            out_shape=local(width, rows),
            in_specs=[VMEM] * (2 * known),
            out_specs=VMEM,
        )(*in_vmem(*sends[:known], *across[:known]))
        bases.append(lax.ppermute(thick, "comp", [(i, i + k) for i in range(comps - k)]))
    cross = call(
        gather_kernel,
        2,
        out_shape=local(8 * depth + 1, width, rows),
        in_specs=[VMEM] * 12,
        out_specs=VMEM,
    )(*in_vmem(near, *bases, *other, *across))
    cross = lax.ppermute(cross, "trc", flip_core)

    count = reaction.shape[0]
    tracers_out, heating = call(
        functools.partial(reaction_kernel, levels),
        6,
        grid=(depth,),
        out_shape=(array(count, depth, width, rows), array(depth, width, rows)),
        in_specs=[SMEM] + [VMEM] * 14,
        out_specs=(
            pl.BlockSpec((count, 1, width, rows), lambda l: (0, l, 0, 0)),
            pl.BlockSpec((1, width, rows), lambda l: (l, 0, 0)),
        ),
        scratch_shapes=[local(width, rows), local(count, width, rows)],
    )(reaction, *in_vmem(sunlight, near, *bases, *mine, *across, cross))
    return (east_out, north_out, tracers_out, heating)


def solution(mesh):
    return jax.shard_map(
        per_device,
        mesh=mesh,
        in_specs=(
            P(("comp", "trc"), None, "horiz", None),
            P(("comp", "trc"), "horiz", None),
            P(("comp", "trc"), "horiz", None),
            P("horiz", None),
            P("horiz", None),
            P(("comp", "trc"), "horiz", None),
            P("horiz", None),
            P(),
        ),
        out_specs=(
            P(("comp", "trc"), "horiz", None),
            P(("comp", "trc"), "horiz", None),
            P(None, ("comp", "trc"), "horiz", None),
            P(("comp", "trc"), "horiz", None),
        ),
        check_vma=False,
    )
```

```python
import functools

import jax
import jax.numpy as jnp
from jax import lax
from jax.experimental import pallas as pl
from jax.experimental.pallas import tpu as pltpu
from jax.sharding import PartitionSpec as P


SUBSTEPS = 4
TIME_STEP = 0.25
VISCOSITY = 0.05
COURANT = 0.2
HALF_LIGHT = 0.3

HALO = 4


SMEM = pl.BlockSpec(memory_space=pltpu.SMEM)
VMEM = pl.BlockSpec(memory_space=pltpu.VMEM)
ANY = pl.BlockSpec(memory_space=pl.ANY)


def local(*shape):
    return pltpu.VMEM(shape, jnp.float32)


def array(*shape):
    return jax.ShapeDtypeStruct(shape, jnp.float32)


def call(kernel, cost, **kwargs):
    return pl.pallas_call(
        kernel,
        compiler_params=pltpu.CompilerParams(vmem_limit_bytes=12 << 20),
        cost_estimate=pl.CostEstimate(flops=cost * 1_000_000, bytes_accessed=cost * 1_000_000, transcendentals=0),
        **kwargs,
    )


def in_hbm(*arrays):
    return [pltpu.with_memory_space_constraint(x, pltpu.HBM) for x in arrays]


def in_vmem(*arrays):
    return [pltpu.with_memory_space_constraint(x, pltpu.VMEM) for x in arrays]


def position():
    return lax.axis_index("comp").astype(jnp.int32), lax.axis_index("trc").astype(jnp.int32)


def shift_of(turn, t):
    if turn < 2:
        return turn
    return jnp.where(t == 0, turn, 5 - turn)


def roll(x, shift, axis):
    return pltpu.roll(x, shift % x.shape[axis], axis)


def segment_copies(field, segment, shift):
    levels = field.shape[0]
    group = segment.shape[0] - 2 * HALO
    comps = levels // group
    c, _ = position()
    start = group * lax.rem(c + shift, comps)
    after = jnp.minimum(start + group, levels - HALO)
    return [
        (field.at[pl.ds(start, group)], segment.at[pl.ds(HALO, group)]),
        (field.at[pl.ds(jnp.maximum(start - HALO, 0), HALO)], segment.at[pl.ds(0, HALO)]),
        (field.at[pl.ds(after, HALO)], segment.at[pl.ds(HALO + group, HALO)]),
    ]


def pack_kernel(field, u, v, k, h, m, one, three, low, high, side_low, side_high, west, east, mask, sem):
    levels, width = field.shape[0], field.shape[1]
    depth = u.shape[0]
    copies = []

    def copy(src, dst):
        copies.append(pltpu.make_async_copy(src, dst, sem.at[len(copies)]))
        copies[-1].start()

    for index, source in enumerate((u, v, k)):
        rows = pl.ds(index * depth, depth)
        copy(source.at[:, width - 8 :, :], low.at[rows])
        copy(source.at[:, :8, :], high.at[rows])
    copy(h.at[width - 8 :, :], low.at[3 * depth])
    copy(h.at[:8, :], high.at[3 * depth])
    copy(m.at[width - 8 :, :], mask.at[0])
    copy(m.at[:8, :], mask.at[1])
    copy(field.at[:, :8, :], west)
    copy(field.at[:, width - 8 :, :], east)
    _, t = position()
    for shift, segment in ((1, one), (shift_of(2, t), three)):
        for src, dst in segment_copies(field, segment, shift):
            copy(src, dst)
    for item in copies[:12]:
        item.wait()
    low[3 * depth + 1] = mask[0].astype(jnp.float32)
    high[3 * depth + 1] = mask[1].astype(jnp.float32)
    half = levels // 2
    upper = lax.broadcasted_iota(jnp.int32, west.shape[1:], 0) < HALO

    def body(level, carry):
        a, b = west[level], west[level + half]
        side_high[level] = jnp.where(upper, a, roll(b, HALO, 0))
        a, b = east[level], east[level + half]
        side_low[level] = jnp.where(upper, roll(b, HALO, 0), a)
        return carry

    lax.fori_loop(0, half, body, 0, unroll=4)
    for item in copies[12:]:
        item.wait()


def side_kernel(field, low, high, own, one, two, three, side, sem):
    levels = side.shape[0]
    half = levels // 2
    width = field.shape[1]
    comps = lax.axis_size("comp")
    group = levels // comps
    c, t = position()
    upper = lax.broadcasted_iota(jnp.int32, side.shape[1:], 0) < HALO
    copies = []
    for shift, segment in ((0, own), (shift_of(3, t), two)):
        for src, dst in segment_copies(field, segment.at[:, :width, :], shift):
            copies.append(pltpu.make_async_copy(src, dst, sem.at[len(copies)]))
            copies[-1].start()

    def body(level, carry):
        a, b = high[level], low[level]
        side[level] = jnp.where(upper, a, b)
        side[level + half] = roll(jnp.where(upper, b, a), HALO, 0)
        return carry

    lax.fori_loop(0, half, body, 0, unroll=4)
    for turn, segment in enumerate((own, one, three, two)):
        start = group * lax.rem(c + shift_of(turn, t), comps)
        columns = slice(width if turn in (0, 3) else 0, None)
        segment[pl.ds(HALO, group), columns, :] = side[pl.ds(start, group)]
        segment[pl.ds(0, HALO), columns, :] = side[pl.ds(jnp.maximum(start - HALO, 0), HALO)]
        segment[pl.ds(HALO + group, HALO), columns, :] = side[pl.ds(jnp.minimum(start + group, levels - HALO), HALO)]
    for item in copies:
        item.wait()


def ocean_kernel(last, u_ref, v_ref, k_ref, h_ref, m_ref, lo_ref, hi_ref, east_ref, north_ref, flux_ref):
    depth, width, rows = u_ref.shape

    def circular(inner, index):
        return jnp.concatenate([inner, hi_ref[index], lo_ref[index]], 0)

    c, t = position()
    first_level = (c * lax.axis_size("trc") + t) * depth
    span = width + 16
    lane = lax.broadcasted_iota(jnp.int32, (span, rows), 1)
    first, final = lane == 0, lane == rows - 1
    east = lambda x: roll(x, -1, 0)
    west = lambda x: roll(x, 1, 0)
    north = lambda x: jnp.where(final, 0.0, roll(x, -1, 1))
    south = lambda x: jnp.where(first, 0.0, roll(x, 1, 1))
    coriolis = 0.5 + 0.5 * lane.astype(jnp.float32) / rows
    h = circular(h_ref[...], 3 * depth)
    wet = circular(m_ref[...].astype(jnp.float32), 3 * depth + 1)
    slope_x = east(h) - h
    slope_y = north(h) - h
    open_x = wet * east(wet)
    open_y = wet * north(wet)
    upper = lax.broadcasted_iota(jnp.int32, (8, rows), 0) < HALO

    def emit(index, level, x):
        flux_ref[index, level, :width, :] = x[:width]
        flux_ref[index, level, width:, :] = jnp.where(upper, x[width : width + 8], x[width + 8 :])

    for level in range(depth):
        u = circular(u_ref[level], level)
        v = circular(v_ref[level], depth + level)
        mixing = circular(k_ref[level], 2 * depth + level)
        lap = east(u) + west(u) + north(u) + south(u) - 4.0 * u
        pair = v + east(v)
        avg = 0.25 * (pair + south(pair))
        east_new = open_x * (u + TIME_STEP * (coriolis * avg - slope_x + VISCOSITY * lap))
        lap = east(v) + west(v) + north(v) + south(v) - 4.0 * v
        pair = u + west(u)
        avg = 0.25 * (pair + north(pair))
        north_new = open_y * (v + TIME_STEP * (-coriolis * avg - slope_y + VISCOSITY * lap))
        speed = jnp.minimum(east_new * east_new + north_new * north_new, 1.0)
        keep = jnp.where(first_level + level < last, 1.0, 0.0)
        kappa = wet * mixing * (1.0 + speed) * keep
        east_ref[level] = east_new[:width]
        north_ref[level] = north_new[:width]
        emit(0, level, COURANT * east_new)
        emit(1, level, COURANT * north_new)
        emit(2, level, kappa)


def weight_kernel(own, core, pair, core_pair, weight_ref):
    depth = own.shape[1]
    _, t = position()
    odd = t & 1

    def fill(position, piece):
        for level in range(depth):
            fx, fy, kappa = piece(0, level), piece(1, level), piece(2, level)
            fw, fs = roll(fx, 1, 0), roll(fy, 1, 1)
            index = position * depth + level
            weight_ref[0, index] = (
                1.0
                - (jnp.maximum(fx, 0.0) - jnp.minimum(fw, 0.0))
                - (jnp.maximum(fy, 0.0) - jnp.minimum(fs, 0.0))
            )
            weight_ref[1, index] = -jnp.minimum(fx, 0.0)
            weight_ref[2, index] = jnp.maximum(fw, 0.0)
            weight_ref[3, index] = -jnp.minimum(fy, 0.0)
            weight_ref[4, index] = jnp.maximum(fs, 0.0)
            weight_ref[5, index] = kappa

    fill(1 + t, lambda i, l: own[i, l])
    fill(1 + (t ^ 1), lambda i, l: core[i, l])
    fill(1 + (t ^ 2), lambda i, l: pair[0, i, l])
    fill(1 + (t ^ 3), lambda i, l: core_pair[0, i, l])
    fill(5 * odd, lambda i, l: pair[1, i, l])
    fill(5 * (1 - odd), lambda i, l: core_pair[1, i, l])


def pair_kernel(across, near, far, out):
    out[0] = across[...]
    out[1] = near[...] + far[...]


def transport_kernel(levels, turn, weight, *refs):
    parts, refs = refs[: 2 - (turn in (0, 3))], refs[2 - (turn in (0, 3)) :]
    if turn == 3:
        earlier, near_ref, refs = refs[:3], refs[3], refs[4:]
    mine_ref, other_ref, send_ref, sums_ref, a, b = refs
    total, _, _ = parts[0].shape
    width = mine_ref.shape[1]
    c, t = position()
    if len(parts) == 2:
        inner, side = parts

        def fill(level, carry):
            a[level, :width, :] = inner[level]
            a[level, width:, :] = side[level]
            return carry

        lax.fori_loop(0, total, fill, 0, unroll=4)
        whole = a
    else:
        whole = parts[0]

    def edge(src, level):
        return weight[5, level] * (src[level + 1] - src[level])

    def update(src, level, above):
        c = src[level]
        below = weight[5, level] * (src[level + 1] - c)
        value = (
            weight[0, level] * c
            + weight[1, level] * roll(c, -1, 0)
            + weight[2, level] * roll(c, 1, 0)
            + weight[3, level] * roll(c, -1, 1)
            + weight[4, level] * roll(c, 1, 1)
            + (below - above)
        )
        return value, below

    for step in range(SUBSTEPS - 1):
        src, dst = (b, a) if step % 2 else (whole if step == 0 else a, b)
        start, stop = step + 1, total - 1 - step

        def body(index, above, src=src, dst=dst, start=start):
            for sub in range(4):
                level = start + 4 * index + sub
                dst[level], above = update(src, level, above)
            return above

        trips = (stop - start) // 4
        above = lax.fori_loop(0, trips, body, edge(src, start - 1))
        for level in range(start + 4 * trips, stop):
            dst[level], above = update(src, level, above)
    src = b if SUBSTEPS % 2 == 0 else a
    outs = (mine_ref, other_ref, send_ref, send_ref)
    for place, out in enumerate(outs):
        block = t ^ place
        first = HALO + HALO * block
        above = edge(src, first - 1)
        tau = None
        for sub in range(HALO):
            value, above = update(src, first + sub, above)
            m = value[:width]
            out[sub + (HALO if place == 3 else 0)] = m
            part = (0.5 + m * m) / levels
            tau = part if tau is None else tau + part
        sums_ref[block] = tau
    zero = jnp.zeros(sums_ref.shape[1:], jnp.float32)

    def thickness(index, *by_comp):
        total = zero
        for holder, part in by_comp:
            total = total + jnp.where((t == 0) & (c == holder), part[index], 0.0)
        return total

    if turn < 3:
        send_ref[2 * HALO] = sum((thickness(index, (turn, sums_ref)) for index in range(4)), zero)
    else:
        running = zero
        for index in range(4):
            if index < 2:
                near_ref[index] = running
            else:
                send_ref[2 * HALO + index - 2] = running
            running = running + thickness(index, *enumerate((*earlier, sums_ref)))


def tau_kernel(*refs):
    sent, received, whole = refs[: len(refs) // 2], refs[len(refs) // 2 : -1], refs[-1]
    _, t = position()
    total = jnp.zeros(whole.shape, jnp.float32)
    for here, there in zip(sent, received):
        total = total + jnp.where(t == 0, here[2 * HALO], jnp.where(t == 2, there[2 * HALO], 0.0))
    whole[...] = total


def gather_kernel(*refs):
    others, across, out = refs[:4], refs[4:6], refs[6]
    depth = others[0].shape[0]
    for index, ref in enumerate(others):
        out[index * depth : (index + 1) * depth] = ref[...]
    for index, ref in enumerate(across):
        out[(4 + index) * depth : (5 + index) * depth] = ref[depth : 2 * depth]


def last_kernel(near, one, two, three, third, fourth, out):
    depth = (out.shape[0] - 1) // 2
    _, t = position()
    out[:depth] = third[depth : 2 * depth]
    out[depth : 2 * depth] = fourth[depth : 2 * depth]
    base = one[...] + two[...] + three[...]
    out[2 * depth] = base + jnp.where(t == 0, near[1], fourth[2 * depth + 1])


def tracer_of(turn, flip):
    c, t = position()
    comps, trcs = lax.axis_size("comp"), lax.axis_size("trc")
    holder = t ^ flip
    return trcs * lax.rem(c + comps - shift_of(turn, holder), comps) + holder


def growth_kernel(terms, react_ref, *refs):
    count, depth, width, _ = refs[-1].shape
    out = refs[-1]
    arrays = max(term[0] for term in terms) + 1
    before = refs[arrays:-1]
    tracers = [tracer_of(turn, flip) for _, _, turn, flip in terms]
    per_level = width // 8

    def chunk(index, carry):
        level = lax.div(index, per_level)
        row = pl.ds(pl.multiple_of(lax.rem(index, per_level) * 8, 8), 8)
        values = [refs[which][start + level, row, :] for which, start, _, _ in terms]
        for i in range(count):
            total = before[0][i, level, row, :] if before else None
            for tracer, value in zip(tracers, values):
                part = react_ref[i, tracer] * value
                total = part if total is None else total + part
            out[i, level, row, :] = total
        return carry

    lax.fori_loop(0, depth * per_level, chunk, 0)


def reaction_kernel(levels, react_ref, sun_ref, near_ref, one, two, three, growth_ref, *refs):
    mine = refs[0:4]
    across = refs[4:8]
    core_ref, last_ref, out_ref, heat_ref, depth, field = refs[8:]
    rows = out_ref.shape[2]
    count = out_ref.shape[0]
    level = pl.program_id(0)
    deep = pl.num_programs(0)
    _, t = position()

    @pl.when(level == 0)
    def _():
        base = one[...] + two[...] + three[...]
        inner = base + jnp.where(t == 0, near_ref[0], across[3][2 * HALO])
        depth[...] = jnp.where(t % 2 == 0, inner, last_ref[2 * deep])

    for turn in range(4):
        field[tracer_of(turn, 0)] = mine[turn][level]
        field[tracer_of(turn, 2)] = across[turn][level]
        field[tracer_of(turn, 1)] = core_ref[turn * deep + level]
        if turn < 2:
            field[tracer_of(turn, 3)] = core_ref[(4 + turn) * deep + level]
        else:
            field[tracer_of(turn, 3)] = last_ref[(turn - 2) * deep + level]
    added = [(tracer_of(2 + part, 3), part) for part in range(2)]

    def chunk(index, carry):
        row = pl.ds(pl.multiple_of(index * 8, 8), 8)
        lead = field[0, row, :]
        tau = (0.5 + lead * lead) / levels
        above = depth[row, :]
        light_top = sun_ref[row, :] * jnp.exp(-above)
        heat_ref[0, row, :] = levels * light_top * (1.0 - jnp.exp(-tau))
        depth[row, :] = above + tau
        light_mid = light_top * jnp.exp(-0.5 * tau)
        limit = light_mid / (light_mid + HALF_LIGHT)
        values = [(tracer, last_ref[part * deep + level, row, :]) for tracer, part in added]
        for i in range(count):
            growth = growth_ref[i, level, row, :]
            for tracer, value in values:
                growth = growth + react_ref[i, tracer] * value
            out_ref[i, 0, row, :] = field[i, row, :] + limit * growth
        return carry

    lax.fori_loop(0, rows // 8, chunk, 0)


def per_device(tracers, eastward, northward, surface_height, sea_mask, mixing, sunlight, reaction):
    i32 = jnp.int32
    depth, width, rows = eastward.shape
    comps, trcs = lax.axis_size("comp"), lax.axis_size("trc")
    tiles = lax.axis_size("horiz")
    levels = depth * comps * trcs
    group = depth * trcs
    tall = group + 2 * HALO
    span = width + 2 * HALO
    forward = [(i, i + 1) for i in range(tiles - 1)]
    backward = [(i + 1, i) for i in range(tiles - 1)]
    flip_x = [(i, i ^ 2) for i in range(trcs)]
    flip_core = [(i, i ^ 1) for i in range(trcs)]
    both = ("comp", "trc")
    edges = 3 * depth + 2

    def ring(*shifts):
        return [
            (trcs * i + j, trcs * ((i + shifts[min(j, len(shifts) - 1)]) % comps) + j)
            for i in range(comps)
            for j in range(trcs)
        ]

    packed = call(
        pack_kernel,
        4,
        out_shape=(local(tall, width, rows),) * 2
        + (local(edges, 8, rows),) * 2
        + (local(levels // 2, 8, rows),) * 2,
        in_specs=[ANY] * 6,
        out_specs=(VMEM,) * 6,
        scratch_shapes=[
            local(levels, 8, rows),
            local(levels, 8, rows),
            pltpu.VMEM((2, 8, rows), i32),
            pltpu.SemaphoreType.DMA((18,)),
        ],
    )(*in_hbm(tracers[0], eastward, northward, mixing, surface_height, sea_mask))
    one, three, low, high, side_low, side_high = packed
    one = lax.ppermute(one, both, ring(1))
    three = lax.ppermute(three, both, ring(2, 3))
    low = lax.ppermute(low, "horiz", forward)
    high = lax.ppermute(high, "horiz", backward)
    side_low = lax.ppermute(side_low, "horiz", forward)
    side_high = lax.ppermute(side_high, "horiz", backward)

    east_out, north_out, flux = call(
        functools.partial(ocean_kernel, levels - 1),
        4,
        out_shape=(array(depth, width, rows),) * 2 + (local(3, depth, span, rows),),
        in_specs=[VMEM] * 7,
        out_specs=(VMEM,) * 3,
    )(eastward, northward, mixing, surface_height, sea_mask, low, high)

    ups = range(comps - 1)
    last, nxt = trcs - 1, trcs
    near = lax.ppermute(
        flux,
        both,
        [(trcs * i + last, trcs * i + nxt + 2) for i in ups] + [(trcs * i + nxt, trcs * i + 1) for i in ups],
    )
    far = lax.ppermute(near, "trc", [(trcs - 2, 0), (1, trcs - 1)])
    across_flux = lax.ppermute(flux, "trc", flip_x)
    core_flux = lax.ppermute(flux, "trc", flip_core)

    whole = local(tall, span, rows)
    flank = local(tall, 8, rows)
    own, side_one, two, side_three = call(
        side_kernel,
        1,
        out_shape=(whole, flank, whole, flank),
        in_specs=[ANY, VMEM, VMEM],
        out_specs=(VMEM,) * 4,
        scratch_shapes=[local(levels, 8, rows), pltpu.SemaphoreType.DMA((6,))],
    )(*in_hbm(tracers[0]), *in_vmem(side_low, side_high))
    side_one = lax.ppermute(side_one, both, ring(1))
    side_three = lax.ppermute(side_three, both, ring(2, 3))
    two = lax.ppermute(two, both, ring(3, 2))
    parts = ((own,), (one, side_one), (three, side_three), (two,))
    pair = call(
        pair_kernel,
        1,
        out_shape=local(2, 3, depth, span, rows),
        in_specs=[VMEM] * 3,
        out_specs=VMEM,
    )(across_flux, near, far)
    core_pair = lax.ppermute(pair, "trc", flip_core)
    weight = call(
        weight_kernel, 3, out_shape=local(6, tall, span, rows), in_specs=[VMEM] * 4, out_specs=VMEM
    )(*in_vmem(flux, core_flux, pair, core_pair))
    piece = local(depth, width, rows)
    mine, other, sends, across, sums = [], [], [], [], []
    for turn in range(4):
        inputs = [weight, *parts[turn]]
        sent = 2 * depth
        if turn == 3:
            inputs += sums
        sent += 2 if turn == 3 else 1
        results = call(
            functools.partial(transport_kernel, levels, turn),
            6,
            out_shape=(local(2, width, rows),) * (turn == 3)
            + (piece, piece, local(sent, width, rows), piece),
            in_specs=[VMEM] * len(inputs),
            out_specs=(VMEM,) * (5 if turn == 3 else 4),
            scratch_shapes=[local(tall, span, rows)] * 2,
        )(*in_vmem(*inputs))
        m, o, held, total = results[-4:]
        mine.append(m)
        other.append(o)
        sends.append(held)
        across.append(lax.ppermute(held, "trc", flip_x))
        sums.append(total)
    near = results[0]
    bases = []
    for k in range(1, comps):
        known = comps - k
        thick = call(
            tau_kernel,
            1,
            out_shape=local(width, rows),
            in_specs=[VMEM] * (2 * known),
            out_specs=VMEM,
        )(*in_vmem(*sends[:known], *across[:known]))
        bases.append(lax.ppermute(thick, "comp", [(i, i + k) for i in range(comps - k)]))
    count = reaction.shape[0]

    def grow(terms, arrays, before=()):
        return call(
            functools.partial(growth_kernel, terms),
            4,
            out_shape=local(count, depth, width, rows),
            in_specs=[SMEM] + [VMEM] * (len(arrays) + len(before)),
            out_specs=VMEM,
        )(reaction, *in_vmem(*arrays, *before))

    cross = call(
        gather_kernel,
        2,
        out_shape=local(6 * depth, width, rows),
        in_specs=[VMEM] * 6,
        out_specs=VMEM,
    )(*in_vmem(*other, *across[:2]))
    cross = lax.ppermute(cross, "trc", flip_core)
    growth = grow(
        tuple((i, 0, i, 0) for i in range(4)) + tuple((4 + i, 0, i, 2) for i in range(2)),
        (*mine, *across[:2]),
    )
    growth = grow(
        tuple((0, i * depth, i, 1) for i in range(4)) + tuple((0, (4 + i) * depth, i, 3) for i in range(2)),
        (cross,),
        (growth,),
    )
    final = call(
        last_kernel,
        1,
        out_shape=local(2 * depth + 1, width, rows),
        in_specs=[VMEM] * 6,
        out_specs=VMEM,
    )(*in_vmem(near, *bases, *across[2:]))
    final = lax.ppermute(final, "trc", flip_core)
    growth = grow(((0, 0, 2, 2), (1, 0, 3, 2)), tuple(across[2:]), (growth,))
    tracers_out, heating = call(
        functools.partial(reaction_kernel, levels),
        6,
        grid=(depth,),
        out_shape=(array(count, depth, width, rows), array(depth, width, rows)),
        in_specs=[SMEM] + [VMEM] * 16,
        out_specs=(
            pl.BlockSpec((count, 1, width, rows), lambda l: (0, l, 0, 0)),
            pl.BlockSpec((1, width, rows), lambda l: (l, 0, 0)),
        ),
        scratch_shapes=[local(width, rows), local(count, width, rows)],
    )(reaction, *in_vmem(sunlight, near, *bases, growth, *mine, *across, cross, final))
    return (east_out, north_out, tracers_out, heating)


def solution(mesh):
    return jax.shard_map(
        per_device,
        mesh=mesh,
        in_specs=(
            P(("comp", "trc"), None, "horiz", None),
            P(("comp", "trc"), "horiz", None),
            P(("comp", "trc"), "horiz", None),
            P("horiz", None),
            P("horiz", None),
            P(("comp", "trc"), "horiz", None),
            P("horiz", None),
            P(),
        ),
        out_specs=(
            P(("comp", "trc"), "horiz", None),
            P(("comp", "trc"), "horiz", None),
            P(None, ("comp", "trc"), "horiz", None),
            P(("comp", "trc"), "horiz", None),
        ),
        check_vma=False,
    )
```

```python
import functools

import jax
import jax.numpy as jnp
from jax import lax
from jax.experimental import pallas as pl
from jax.experimental.pallas import tpu as pltpu
from jax.sharding import PartitionSpec as P


SUBSTEPS = 4
TIME_STEP = 0.25
VISCOSITY = 0.05
COURANT = 0.2
HALF_LIGHT = 0.3

HALO = 4


SMEM = pl.BlockSpec(memory_space=pltpu.SMEM)
VMEM = pl.BlockSpec(memory_space=pltpu.VMEM)
ANY = pl.BlockSpec(memory_space=pl.ANY)


def local(*shape):
    return pltpu.VMEM(shape, jnp.float32)


def array(*shape):
    return jax.ShapeDtypeStruct(shape, jnp.float32)


def call(kernel, cost, **kwargs):
    return pl.pallas_call(
        kernel,
        compiler_params=pltpu.CompilerParams(vmem_limit_bytes=12 << 20),
        cost_estimate=pl.CostEstimate(flops=cost * 1_000_000, bytes_accessed=cost * 1_000_000, transcendentals=0),
        **kwargs,
    )


def in_hbm(*arrays):
    return [pltpu.with_memory_space_constraint(x, pltpu.HBM) for x in arrays]


def in_vmem(*arrays):
    return [pltpu.with_memory_space_constraint(x, pltpu.VMEM) for x in arrays]


def position():
    return lax.axis_index("comp").astype(jnp.int32), lax.axis_index("trc").astype(jnp.int32)


def shift_of(turn, t):
    if turn < 2:
        return turn
    return jnp.where(t == 0, turn, 5 - turn)


def roll(x, shift, axis):
    return pltpu.roll(x, shift % x.shape[axis], axis)


def segment_copies(field, segment, shift):
    levels = field.shape[0]
    group = segment.shape[0] - 2 * HALO
    comps = levels // group
    c, _ = position()
    start = group * lax.rem(c + shift, comps)
    after = jnp.minimum(start + group, levels - HALO)
    return [
        (field.at[pl.ds(start, group)], segment.at[pl.ds(HALO, group)]),
        (field.at[pl.ds(jnp.maximum(start - HALO, 0), HALO)], segment.at[pl.ds(0, HALO)]),
        (field.at[pl.ds(after, HALO)], segment.at[pl.ds(HALO + group, HALO)]),
    ]


def pack_kernel(field, u, v, k, h, m, one, three, low, high, side_low, side_high, west, east, mask, sem):
    levels, width = field.shape[0], field.shape[1]
    depth = u.shape[0]
    copies = []

    def copy(src, dst):
        copies.append(pltpu.make_async_copy(src, dst, sem.at[len(copies)]))
        copies[-1].start()

    for index, source in enumerate((u, v, k)):
        rows = pl.ds(index * depth, depth)
        copy(source.at[:, width - 8 :, :], low.at[rows])
        copy(source.at[:, :8, :], high.at[rows])
    copy(h.at[width - 8 :, :], low.at[3 * depth])
    copy(h.at[:8, :], high.at[3 * depth])
    copy(m.at[width - 8 :, :], mask.at[0])
    copy(m.at[:8, :], mask.at[1])
    copy(field.at[:, :8, :], west)
    copy(field.at[:, width - 8 :, :], east)
    _, t = position()
    for shift, segment in ((1, one), (shift_of(2, t), three)):
        for src, dst in segment_copies(field, segment, shift):
            copy(src, dst)
    for item in copies[:12]:
        item.wait()
    low[3 * depth + 1] = mask[0].astype(jnp.float32)
    high[3 * depth + 1] = mask[1].astype(jnp.float32)
    half = levels // 2
    upper = lax.broadcasted_iota(jnp.int32, west.shape[1:], 0) < HALO

    def body(level, carry):
        a, b = west[level], west[level + half]
        side_high[level] = jnp.where(upper, a, roll(b, HALO, 0))
        a, b = east[level], east[level + half]
        side_low[level] = jnp.where(upper, roll(b, HALO, 0), a)
        return carry

    lax.fori_loop(0, half, body, 0, unroll=4)
    for item in copies[12:]:
        item.wait()


def side_kernel(field, low, high, own, one, two, three, side, sem):
    levels = side.shape[0]
    half = levels // 2
    width = field.shape[1]
    comps = lax.axis_size("comp")
    group = levels // comps
    c, t = position()
    upper = lax.broadcasted_iota(jnp.int32, side.shape[1:], 0) < HALO
    copies = []
    for shift, segment in ((0, own), (shift_of(3, t), two)):
        for src, dst in segment_copies(field, segment.at[:, :width, :], shift):
            copies.append(pltpu.make_async_copy(src, dst, sem.at[len(copies)]))
            copies[-1].start()

    def body(level, carry):
        a, b = high[level], low[level]
        side[level] = jnp.where(upper, a, b)
        side[level + half] = roll(jnp.where(upper, b, a), HALO, 0)
        return carry

    lax.fori_loop(0, half, body, 0, unroll=4)
    for turn, segment in enumerate((own, one, three, two)):
        start = group * lax.rem(c + shift_of(turn, t), comps)
        columns = slice(width if turn in (0, 3) else 0, None)
        segment[pl.ds(HALO, group), columns, :] = side[pl.ds(start, group)]
        segment[pl.ds(0, HALO), columns, :] = side[pl.ds(jnp.maximum(start - HALO, 0), HALO)]
        segment[pl.ds(HALO + group, HALO), columns, :] = side[pl.ds(jnp.minimum(start + group, levels - HALO), HALO)]
    for item in copies:
        item.wait()


def ocean_kernel(last, u_ref, v_ref, k_ref, h_ref, m_ref, lo_ref, hi_ref, east_ref, north_ref, flux_ref):
    depth, width, rows = u_ref.shape

    def circular(inner, index):
        return jnp.concatenate([inner, hi_ref[index], lo_ref[index]], 0)

    c, t = position()
    first_level = (c * lax.axis_size("trc") + t) * depth
    span = width + 16
    lane = lax.broadcasted_iota(jnp.int32, (span, rows), 1)
    first, final = lane == 0, lane == rows - 1
    east = lambda x: roll(x, -1, 0)
    west = lambda x: roll(x, 1, 0)
    north = lambda x: jnp.where(final, 0.0, roll(x, -1, 1))
    south = lambda x: jnp.where(first, 0.0, roll(x, 1, 1))
    coriolis = 0.5 + 0.5 * lane.astype(jnp.float32) / rows
    h = circular(h_ref[...], 3 * depth)
    wet = circular(m_ref[...].astype(jnp.float32), 3 * depth + 1)
    slope_x = east(h) - h
    slope_y = north(h) - h
    open_x = wet * east(wet)
    open_y = wet * north(wet)
    upper = lax.broadcasted_iota(jnp.int32, (8, rows), 0) < HALO

    def emit(index, level, x):
        flux_ref[index, level, :width, :] = x[:width]
        flux_ref[index, level, width:, :] = jnp.where(upper, x[width : width + 8], x[width + 8 :])

    for level in range(depth):
        u = circular(u_ref[level], level)
        v = circular(v_ref[level], depth + level)
        mixing = circular(k_ref[level], 2 * depth + level)
        lap = east(u) + west(u) + north(u) + south(u) - 4.0 * u
        pair = v + east(v)
        avg = 0.25 * (pair + south(pair))
        east_new = open_x * (u + TIME_STEP * (coriolis * avg - slope_x + VISCOSITY * lap))
        lap = east(v) + west(v) + north(v) + south(v) - 4.0 * v
        pair = u + west(u)
        avg = 0.25 * (pair + north(pair))
        north_new = open_y * (v + TIME_STEP * (-coriolis * avg - slope_y + VISCOSITY * lap))
        speed = jnp.minimum(east_new * east_new + north_new * north_new, 1.0)
        keep = jnp.where(first_level + level < last, 1.0, 0.0)
        kappa = wet * mixing * (1.0 + speed) * keep
        east_ref[level] = east_new[:width]
        north_ref[level] = north_new[:width]
        emit(0, level, COURANT * east_new)
        emit(1, level, COURANT * north_new)
        emit(2, level, kappa)


def weight_kernel(own, across, core, rim, core_rim, weight_ref):
    depth = own.shape[1]
    _, t = position()
    odd = t & 1

    def fill(position, piece):
        for level in range(depth):
            fx, fy, kappa = piece(0, level), piece(1, level), piece(2, level)
            fw, fs = roll(fx, 1, 0), roll(fy, 1, 1)
            index = position * depth + level
            weight_ref[0, index] = (
                1.0
                - (jnp.maximum(fx, 0.0) - jnp.minimum(fw, 0.0))
                - (jnp.maximum(fy, 0.0) - jnp.minimum(fs, 0.0))
            )
            weight_ref[1, index] = -jnp.minimum(fx, 0.0)
            weight_ref[2, index] = jnp.maximum(fw, 0.0)
            weight_ref[3, index] = -jnp.minimum(fy, 0.0)
            weight_ref[4, index] = jnp.maximum(fs, 0.0)
            weight_ref[5, index] = kappa

    fill(1 + t, lambda i, l: own[i, l])
    fill(1 + (t ^ 1), lambda i, l: core[0, i, l])
    fill(1 + (t ^ 2), lambda i, l: across[i, l])
    fill(1 + (t ^ 3), lambda i, l: core[1, i, l])
    fill(5 * odd, lambda i, l: rim[i, l])
    fill(5 * (1 - odd), lambda i, l: core_rim[i, l])


def pair_kernel(own, across, out):
    out[0] = own[...]
    out[1] = across[...]


def rim_kernel(near, far, out):
    out[...] = near[...] + far[...]


def transport_kernel(levels, turn, weight, *refs):
    parts, refs = refs[: 2 - (turn in (0, 3))], refs[2 - (turn in (0, 3)) :]
    if turn == 3:
        earlier, near_ref, refs = refs[:3], refs[3], refs[4:]
    mine_ref, other_ref, send_ref, sums_ref, a, b = refs
    total, _, _ = parts[0].shape
    width = mine_ref.shape[1]
    c, t = position()
    if len(parts) == 2:
        inner, side = parts

        def fill(level, carry):
            a[level, :width, :] = inner[level]
            a[level, width:, :] = side[level]
            return carry

        lax.fori_loop(0, total, fill, 0, unroll=4)
        whole = a
    else:
        whole = parts[0]

    def edge(src, level):
        return weight[5, level] * (src[level + 1] - src[level])

    def update(src, level, above):
        c = src[level]
        below = weight[5, level] * (src[level + 1] - c)
        value = (
            weight[0, level] * c
            + weight[1, level] * roll(c, -1, 0)
            + weight[2, level] * roll(c, 1, 0)
            + weight[3, level] * roll(c, -1, 1)
            + weight[4, level] * roll(c, 1, 1)
            + (below - above)
        )
        return value, below

    for step in range(SUBSTEPS - 1):
        src, dst = (b, a) if step % 2 else (whole if step == 0 else a, b)
        start, stop = step + 1, total - 1 - step

        def body(index, above, src=src, dst=dst, start=start):
            for sub in range(4):
                level = start + 4 * index + sub
                dst[level], above = update(src, level, above)
            return above

        trips = (stop - start) // 4
        above = lax.fori_loop(0, trips, body, edge(src, start - 1))
        for level in range(start + 4 * trips, stop):
            dst[level], above = update(src, level, above)
    src = b if SUBSTEPS % 2 == 0 else a
    outs = (mine_ref, other_ref, send_ref, send_ref)
    for place, out in enumerate(outs):
        block = t ^ place
        first = HALO + HALO * block
        above = edge(src, first - 1)
        tau = None
        for sub in range(HALO):
            value, above = update(src, first + sub, above)
            m = value[:width]
            out[sub + (HALO if place == 3 else 0)] = m
            part = (0.5 + m * m) / levels
            tau = part if tau is None else tau + part
        sums_ref[block] = tau
    zero = jnp.zeros(sums_ref.shape[1:], jnp.float32)

    def thickness(index, *by_comp):
        total = zero
        for holder, part in by_comp:
            total = total + jnp.where((t == 0) & (c == holder), part[index], 0.0)
        return total

    if turn < 3:
        send_ref[2 * HALO] = sum((thickness(index, (turn, sums_ref)) for index in range(4)), zero)
    else:
        running = zero
        for index in range(4):
            if index < 2:
                near_ref[index] = running
            else:
                send_ref[2 * HALO + index - 2] = running
            running = running + thickness(index, *enumerate((*earlier, sums_ref)))


def tau_kernel(*refs):
    sent, received, whole = refs[: len(refs) // 2], refs[len(refs) // 2 : -1], refs[-1]
    _, t = position()
    total = jnp.zeros(whole.shape, jnp.float32)
    for here, there in zip(sent, received):
        total = total + jnp.where(t == 0, here[2 * HALO], jnp.where(t == 2, there[2 * HALO], 0.0))
    whole[...] = total


def gather_kernel(*refs):
    others, across, out = refs[:4], refs[4:6], refs[6]
    depth = others[0].shape[0]
    for index, ref in enumerate(others):
        out[index * depth : (index + 1) * depth] = ref[...]
    for index, ref in enumerate(across):
        out[(4 + index) * depth : (5 + index) * depth] = ref[depth : 2 * depth]


def last_kernel(near, one, two, three, third, fourth, out):
    depth = (out.shape[0] - 1) // 2
    _, t = position()
    out[:depth] = third[depth : 2 * depth]
    out[depth : 2 * depth] = fourth[depth : 2 * depth]
    base = one[...] + two[...] + three[...]
    out[2 * depth] = base + jnp.where(t == 0, near[1], fourth[2 * depth + 1])


def tracer_of(turn, flip):
    c, t = position()
    comps, trcs = lax.axis_size("comp"), lax.axis_size("trc")
    holder = t ^ flip
    return trcs * lax.rem(c + comps - shift_of(turn, holder), comps) + holder


def growth_kernel(terms, react_ref, *refs):
    count, depth, width, _ = refs[-1].shape
    out = refs[-1]
    arrays = max(term[0] for term in terms) + 1
    before = refs[arrays:-1]
    tracers = [tracer_of(turn, flip) for _, _, turn, flip in terms]
    per_level = width // 8

    def chunk(index, carry):
        level = lax.div(index, per_level)
        row = pl.ds(pl.multiple_of(lax.rem(index, per_level) * 8, 8), 8)
        values = [refs[which][start + level, row, :] for which, start, _, _ in terms]
        for i in range(count):
            total = before[0][i, level, row, :] if before else None
            for tracer, value in zip(tracers, values):
                part = react_ref[i, tracer] * value
                total = part if total is None else total + part
            out[i, level, row, :] = total
        return carry

    lax.fori_loop(0, depth * per_level, chunk, 0)


def reaction_kernel(levels, react_ref, sun_ref, near_ref, one, two, three, growth_ref, *refs):
    mine = refs[0:4]
    across = refs[4:8]
    core_ref, last_ref, out_ref, heat_ref, depth, field = refs[8:]
    rows = out_ref.shape[2]
    count = out_ref.shape[0]
    level = pl.program_id(0)
    deep = pl.num_programs(0)
    _, t = position()

    @pl.when(level == 0)
    def _():
        base = one[...] + two[...] + three[...]
        inner = base + jnp.where(t == 0, near_ref[0], across[3][2 * HALO])
        depth[...] = jnp.where(t % 2 == 0, inner, last_ref[2 * deep])

    for turn in range(4):
        field[tracer_of(turn, 0)] = mine[turn][level]
        field[tracer_of(turn, 2)] = across[turn][level]
        field[tracer_of(turn, 1)] = core_ref[turn * deep + level]
        if turn < 2:
            field[tracer_of(turn, 3)] = core_ref[(4 + turn) * deep + level]
        else:
            field[tracer_of(turn, 3)] = last_ref[(turn - 2) * deep + level]
    added = [(tracer_of(2 + part, 3), part) for part in range(2)]

    def chunk(index, carry):
        row = pl.ds(pl.multiple_of(index * 8, 8), 8)
        lead = field[0, row, :]
        tau = (0.5 + lead * lead) / levels
        above = depth[row, :]
        light_top = sun_ref[row, :] * jnp.exp(-above)
        heat_ref[0, row, :] = levels * light_top * (1.0 - jnp.exp(-tau))
        depth[row, :] = above + tau
        light_mid = light_top * jnp.exp(-0.5 * tau)
        limit = light_mid / (light_mid + HALF_LIGHT)
        values = [(tracer, last_ref[part * deep + level, row, :]) for tracer, part in added]
        for i in range(count):
            growth = growth_ref[i, level, row, :]
            for tracer, value in values:
                growth = growth + react_ref[i, tracer] * value
            out_ref[i, 0, row, :] = field[i, row, :] + limit * growth
        return carry

    lax.fori_loop(0, rows // 8, chunk, 0)


def per_device(tracers, eastward, northward, surface_height, sea_mask, mixing, sunlight, reaction):
    i32 = jnp.int32
    depth, width, rows = eastward.shape
    comps, trcs = lax.axis_size("comp"), lax.axis_size("trc")
    tiles = lax.axis_size("horiz")
    levels = depth * comps * trcs
    group = depth * trcs
    tall = group + 2 * HALO
    span = width + 2 * HALO
    forward = [(i, i + 1) for i in range(tiles - 1)]
    backward = [(i + 1, i) for i in range(tiles - 1)]
    flip_x = [(i, i ^ 2) for i in range(trcs)]
    flip_core = [(i, i ^ 1) for i in range(trcs)]
    both = ("comp", "trc")
    edges = 3 * depth + 2

    def ring(*shifts):
        return [
            (trcs * i + j, trcs * ((i + shifts[min(j, len(shifts) - 1)]) % comps) + j)
            for i in range(comps)
            for j in range(trcs)
        ]

    packed = call(
        pack_kernel,
        4,
        out_shape=(local(tall, width, rows),) * 2
        + (local(edges, 8, rows),) * 2
        + (local(levels // 2, 8, rows),) * 2,
        in_specs=[ANY] * 6,
        out_specs=(VMEM,) * 6,
        scratch_shapes=[
            local(levels, 8, rows),
            local(levels, 8, rows),
            pltpu.VMEM((2, 8, rows), i32),
            pltpu.SemaphoreType.DMA((18,)),
        ],
    )(*in_hbm(tracers[0], eastward, northward, mixing, surface_height, sea_mask))
    one, three, low, high, side_low, side_high = packed
    one = lax.ppermute(one, both, ring(1))
    three = lax.ppermute(three, both, ring(2, 3))
    low = lax.ppermute(low, "horiz", forward)
    high = lax.ppermute(high, "horiz", backward)
    side_low = lax.ppermute(side_low, "horiz", forward)
    side_high = lax.ppermute(side_high, "horiz", backward)

    east_out, north_out, flux = call(
        functools.partial(ocean_kernel, levels - 1),
        4,
        out_shape=(array(depth, width, rows),) * 2 + (local(3, depth, span, rows),),
        in_specs=[VMEM] * 7,
        out_specs=(VMEM,) * 3,
    )(eastward, northward, mixing, surface_height, sea_mask, low, high)

    ups = range(comps - 1)
    last, nxt = trcs - 1, trcs
    near = lax.ppermute(
        flux,
        both,
        [(trcs * i + last, trcs * i + nxt + 2) for i in ups] + [(trcs * i + nxt, trcs * i + 1) for i in ups],
    )
    far = lax.ppermute(near, "trc", [(trcs - 2, 0), (1, trcs - 1)])
    across_flux = lax.ppermute(flux, "trc", flip_x)

    whole = local(tall, span, rows)
    flank = local(tall, 8, rows)
    own, side_one, two, side_three = call(
        side_kernel,
        1,
        out_shape=(whole, flank, whole, flank),
        in_specs=[ANY, VMEM, VMEM],
        out_specs=(VMEM,) * 4,
        scratch_shapes=[local(levels, 8, rows), pltpu.SemaphoreType.DMA((6,))],
    )(*in_hbm(tracers[0]), *in_vmem(side_low, side_high))
    side_one = lax.ppermute(side_one, both, ring(1))
    side_three = lax.ppermute(side_three, both, ring(2, 3))
    two = lax.ppermute(two, both, ring(3, 2))
    parts = ((own,), (one, side_one), (three, side_three), (two,))
    pair = call(
        pair_kernel,
        1,
        out_shape=local(2, 3, depth, span, rows),
        in_specs=[VMEM] * 2,
        out_specs=VMEM,
    )(*in_vmem(flux, across_flux))
    core_flux = lax.ppermute(pair, "trc", flip_core)
    rim = call(
        rim_kernel, 1, out_shape=local(3, depth, span, rows), in_specs=[VMEM] * 2, out_specs=VMEM
    )(*in_vmem(near, far))
    core_rim = lax.ppermute(rim, "trc", flip_core)
    weight = call(
        weight_kernel, 3, out_shape=local(6, tall, span, rows), in_specs=[VMEM] * 5, out_specs=VMEM
    )(*in_vmem(flux, across_flux, core_flux, rim, core_rim))
    piece = local(depth, width, rows)
    mine, other, sends, across, sums = [], [], [], [], []
    for turn in range(4):
        inputs = [weight, *parts[turn]]
        sent = 2 * depth
        if turn == 3:
            inputs += sums
        sent += 2 if turn == 3 else 1
        results = call(
            functools.partial(transport_kernel, levels, turn),
            6,
            out_shape=(local(2, width, rows),) * (turn == 3)
            + (piece, piece, local(sent, width, rows), piece),
            in_specs=[VMEM] * len(inputs),
            out_specs=(VMEM,) * (5 if turn == 3 else 4),
            scratch_shapes=[local(tall, span, rows)] * 2,
        )(*in_vmem(*inputs))
        m, o, held, total = results[-4:]
        mine.append(m)
        other.append(o)
        sends.append(held)
        across.append(lax.ppermute(held, "trc", flip_x))
        sums.append(total)
    near = results[0]
    bases = []
    for k in range(1, comps):
        known = comps - k
        thick = call(
            tau_kernel,
            1,
            out_shape=local(width, rows),
            in_specs=[VMEM] * (2 * known),
            out_specs=VMEM,
        )(*in_vmem(*sends[:known], *across[:known]))
        bases.append(lax.ppermute(thick, "comp", [(i, i + k) for i in range(comps - k)]))
    count = reaction.shape[0]

    def grow(terms, arrays, before=()):
        return call(
            functools.partial(growth_kernel, terms),
            4,
            out_shape=local(count, depth, width, rows),
            in_specs=[SMEM] + [VMEM] * (len(arrays) + len(before)),
            out_specs=VMEM,
        )(reaction, *in_vmem(*arrays, *before))

    cross = call(
        gather_kernel,
        2,
        out_shape=local(6 * depth, width, rows),
        in_specs=[VMEM] * 6,
        out_specs=VMEM,
    )(*in_vmem(*other, *across[:2]))
    cross = lax.ppermute(cross, "trc", flip_core)
    growth = grow(
        tuple((i, 0, i, 0) for i in range(4)) + tuple((4 + i, 0, i, 2) for i in range(2)),
        (*mine, *across[:2]),
    )
    growth = grow(
        tuple((0, i * depth, i, 1) for i in range(4)) + tuple((0, (4 + i) * depth, i, 3) for i in range(2)),
        (cross,),
        (growth,),
    )
    final = call(
        last_kernel,
        1,
        out_shape=local(2 * depth + 1, width, rows),
        in_specs=[VMEM] * 6,
        out_specs=VMEM,
    )(*in_vmem(near, *bases, *across[2:]))
    final = lax.ppermute(final, "trc", flip_core)
    growth = grow(((0, 0, 2, 2), (1, 0, 3, 2)), tuple(across[2:]), (growth,))
    tracers_out, heating = call(
        functools.partial(reaction_kernel, levels),
        6,
        grid=(depth,),
        out_shape=(array(count, depth, width, rows), array(depth, width, rows)),
        in_specs=[SMEM] + [VMEM] * 16,
        out_specs=(
            pl.BlockSpec((count, 1, width, rows), lambda l: (0, l, 0, 0)),
            pl.BlockSpec((1, width, rows), lambda l: (l, 0, 0)),
        ),
        scratch_shapes=[local(width, rows), local(count, width, rows)],
    )(reaction, *in_vmem(sunlight, near, *bases, growth, *mine, *across, cross, final))
    return (east_out, north_out, tracers_out, heating)


def solution(mesh):
    return jax.shard_map(
        per_device,
        mesh=mesh,
        in_specs=(
            P(("comp", "trc"), None, "horiz", None),
            P(("comp", "trc"), "horiz", None),
            P(("comp", "trc"), "horiz", None),
            P("horiz", None),
            P("horiz", None),
            P(("comp", "trc"), "horiz", None),
            P("horiz", None),
            P(),
        ),
        out_specs=(
            P(("comp", "trc"), "horiz", None),
            P(("comp", "trc"), "horiz", None),
            P(None, ("comp", "trc"), "horiz", None),
            P(("comp", "trc"), "horiz", None),
        ),
        check_vma=False,
    )
```

```python
import functools

import jax
import jax.numpy as jnp
from jax import lax
from jax.experimental import pallas as pl
from jax.experimental.pallas import tpu as pltpu
from jax.sharding import PartitionSpec as P


SUBSTEPS = 4
TIME_STEP = 0.25
VISCOSITY = 0.05
COURANT = 0.2
HALF_LIGHT = 0.3

HALO = 4


SMEM = pl.BlockSpec(memory_space=pltpu.SMEM)
VMEM = pl.BlockSpec(memory_space=pltpu.VMEM)
ANY = pl.BlockSpec(memory_space=pl.ANY)


def local(*shape):
    return pltpu.VMEM(shape, jnp.float32)


def array(*shape):
    return jax.ShapeDtypeStruct(shape, jnp.float32)


def call(kernel, cost, **kwargs):
    return pl.pallas_call(
        kernel,
        compiler_params=pltpu.CompilerParams(vmem_limit_bytes=12 << 20),
        cost_estimate=pl.CostEstimate(flops=cost * 1_000_000, bytes_accessed=cost * 1_000_000, transcendentals=0),
        **kwargs,
    )


def in_hbm(*arrays):
    return [pltpu.with_memory_space_constraint(x, pltpu.HBM) for x in arrays]


def in_vmem(*arrays):
    return [pltpu.with_memory_space_constraint(x, pltpu.VMEM) for x in arrays]


def position():
    return lax.axis_index("comp").astype(jnp.int32), lax.axis_index("trc").astype(jnp.int32)


def shift_of(turn, t):
    if turn < 2:
        return turn
    return jnp.where(t == 0, turn, 5 - turn)


def roll(x, shift, axis):
    return pltpu.roll(x, shift % x.shape[axis], axis)


def segment_copies(field, segment, shift):
    levels = field.shape[0]
    group = segment.shape[0] - 2 * HALO
    comps = levels // group
    c, _ = position()
    start = group * lax.rem(c + shift, comps)
    after = jnp.minimum(start + group, levels - HALO)
    return [
        (field.at[pl.ds(start, group)], segment.at[pl.ds(HALO, group)]),
        (field.at[pl.ds(jnp.maximum(start - HALO, 0), HALO)], segment.at[pl.ds(0, HALO)]),
        (field.at[pl.ds(after, HALO)], segment.at[pl.ds(HALO + group, HALO)]),
    ]


def pack_kernel(field, u, v, k, h, m, one, three, low, high, side_low, side_high, west, east, mask, sem):
    levels, width = field.shape[0], field.shape[1]
    depth = u.shape[0]
    copies = []

    def copy(src, dst):
        copies.append(pltpu.make_async_copy(src, dst, sem.at[len(copies)]))
        copies[-1].start()

    for index, source in enumerate((u, v, k)):
        rows = pl.ds(index * depth, depth)
        copy(source.at[:, width - 8 :, :], low.at[rows])
        copy(source.at[:, :8, :], high.at[rows])
    copy(h.at[width - 8 :, :], low.at[3 * depth])
    copy(h.at[:8, :], high.at[3 * depth])
    copy(m.at[width - 8 :, :], mask.at[0])
    copy(m.at[:8, :], mask.at[1])
    copy(field.at[:, :8, :], west)
    copy(field.at[:, width - 8 :, :], east)
    _, t = position()
    for shift, segment in ((1, one), (shift_of(2, t), three)):
        for src, dst in segment_copies(field, segment, shift):
            copy(src, dst)
    for item in copies[:12]:
        item.wait()
    low[3 * depth + 1] = mask[0].astype(jnp.float32)
    high[3 * depth + 1] = mask[1].astype(jnp.float32)
    half = levels // 2
    upper = lax.broadcasted_iota(jnp.int32, west.shape[1:], 0) < HALO

    def body(level, carry):
        a, b = west[level], west[level + half]
        side_high[level] = jnp.where(upper, a, roll(b, HALO, 0))
        a, b = east[level], east[level + half]
        side_low[level] = jnp.where(upper, roll(b, HALO, 0), a)
        return carry

    lax.fori_loop(0, half, body, 0, unroll=4)
    for item in copies[12:]:
        item.wait()


def side_kernel(field, low, high, own, one, two, three, side, sem):
    levels = side.shape[0]
    half = levels // 2
    width = field.shape[1]
    comps = lax.axis_size("comp")
    group = levels // comps
    c, t = position()
    upper = lax.broadcasted_iota(jnp.int32, side.shape[1:], 0) < HALO
    copies = []
    for shift, segment in ((0, own), (shift_of(3, t), two)):
        for src, dst in segment_copies(field, segment.at[:, :width, :], shift):
            copies.append(pltpu.make_async_copy(src, dst, sem.at[len(copies)]))
            copies[-1].start()

    def body(level, carry):
        a, b = high[level], low[level]
        side[level] = jnp.where(upper, a, b)
        side[level + half] = roll(jnp.where(upper, b, a), HALO, 0)
        return carry

    lax.fori_loop(0, half, body, 0, unroll=4)
    for turn, segment in enumerate((own, one, three, two)):
        start = group * lax.rem(c + shift_of(turn, t), comps)
        columns = slice(width if turn in (0, 3) else 0, None)
        segment[pl.ds(HALO, group), columns, :] = side[pl.ds(start, group)]
        segment[pl.ds(0, HALO), columns, :] = side[pl.ds(jnp.maximum(start - HALO, 0), HALO)]
        segment[pl.ds(HALO + group, HALO), columns, :] = side[pl.ds(jnp.minimum(start + group, levels - HALO), HALO)]
    for item in copies:
        item.wait()


def ocean_kernel(last, u_ref, v_ref, k_ref, h_ref, m_ref, lo_ref, hi_ref, east_ref, north_ref, flux_ref):
    depth, width, rows = u_ref.shape

    def circular(inner, index):
        return jnp.concatenate([inner, hi_ref[index], lo_ref[index]], 0)

    c, t = position()
    first_level = (c * lax.axis_size("trc") + t) * depth
    span = width + 16
    lane = lax.broadcasted_iota(jnp.int32, (span, rows), 1)
    first, final = lane == 0, lane == rows - 1
    east = lambda x: roll(x, -1, 0)
    west = lambda x: roll(x, 1, 0)
    north = lambda x: jnp.where(final, 0.0, roll(x, -1, 1))
    south = lambda x: jnp.where(first, 0.0, roll(x, 1, 1))
    coriolis = 0.5 + 0.5 * lane.astype(jnp.float32) / rows
    h = circular(h_ref[...], 3 * depth)
    wet = circular(m_ref[...].astype(jnp.float32), 3 * depth + 1)
    slope_x = east(h) - h
    slope_y = north(h) - h
    open_x = wet * east(wet)
    open_y = wet * north(wet)
    upper = lax.broadcasted_iota(jnp.int32, (8, rows), 0) < HALO

    def emit(index, level, x):
        flux_ref[index, level, :width, :] = x[:width]
        flux_ref[index, level, width:, :] = jnp.where(upper, x[width : width + 8], x[width + 8 :])

    for level in range(depth):
        u = circular(u_ref[level], level)
        v = circular(v_ref[level], depth + level)
        mixing = circular(k_ref[level], 2 * depth + level)
        lap = east(u) + west(u) + north(u) + south(u) - 4.0 * u
        pair = v + east(v)
        avg = 0.25 * (pair + south(pair))
        east_new = open_x * (u + TIME_STEP * (coriolis * avg - slope_x + VISCOSITY * lap))
        lap = east(v) + west(v) + north(v) + south(v) - 4.0 * v
        pair = u + west(u)
        avg = 0.25 * (pair + north(pair))
        north_new = open_y * (v + TIME_STEP * (-coriolis * avg - slope_y + VISCOSITY * lap))
        speed = jnp.minimum(east_new * east_new + north_new * north_new, 1.0)
        keep = jnp.where(first_level + level < last, 1.0, 0.0)
        kappa = wet * mixing * (1.0 + speed) * keep
        east_ref[level] = east_new[:width]
        north_ref[level] = north_new[:width]
        emit(0, level, COURANT * east_new)
        emit(1, level, COURANT * north_new)
        emit(2, level, kappa)


def weight_kernel(*refs):
    pieces, weight_ref = refs[:-1], refs[-1]
    depth = pieces[-1].shape[-3]
    _, t = position()
    odd = t & 1

    def fill(position, piece):
        for level in range(depth):
            fx, fy, kappa = piece(0, level), piece(1, level), piece(2, level)
            fw, fs = roll(fx, 1, 0), roll(fy, 1, 1)
            index = position * depth + level
            weight_ref[0, index] = (
                1.0
                - (jnp.maximum(fx, 0.0) - jnp.minimum(fw, 0.0))
                - (jnp.maximum(fy, 0.0) - jnp.minimum(fs, 0.0))
            )
            weight_ref[1, index] = -jnp.minimum(fx, 0.0)
            weight_ref[2, index] = jnp.maximum(fw, 0.0)
            weight_ref[3, index] = -jnp.minimum(fy, 0.0)
            weight_ref[4, index] = jnp.maximum(fs, 0.0)
            weight_ref[5, index] = kappa

    if len(pieces) == 2:
        own, core = pieces
        fill(1 + t, lambda i, l: own[0, i, l])
        fill(1 + (t ^ 2), lambda i, l: own[1, i, l])
        fill(1 + (t ^ 1), lambda i, l: core[0, i, l])
        fill(1 + (t ^ 3), lambda i, l: core[1, i, l])
    else:
        _, rim, core_rim = pieces
        fill(5 * odd, lambda i, l: rim[i, l])
        fill(5 * (1 - odd), lambda i, l: core_rim[i, l])


def pair_kernel(own, across, out):
    out[0] = own[...]
    out[1] = across[...]


def rim_kernel(near, far, out):
    out[...] = near[...] + far[...]


def transport_kernel(levels, turn, weight, *refs):
    parts, refs = refs[: 2 - (turn in (0, 3))], refs[2 - (turn in (0, 3)) :]
    if turn == 3:
        earlier, near_ref, refs = refs[:3], refs[3], refs[4:]
    mine_ref, other_ref, send_ref, sums_ref, a, b = refs
    total, _, _ = parts[0].shape
    width = mine_ref.shape[1]
    c, t = position()
    if len(parts) == 2:
        inner, side = parts

        def fill(level, carry):
            a[level, :width, :] = inner[level]
            a[level, width:, :] = side[level]
            return carry

        lax.fori_loop(0, total, fill, 0, unroll=4)
        whole = a
    else:
        whole = parts[0]

    def edge(src, level):
        return weight[5, level] * (src[level + 1] - src[level])

    def update(src, level, above):
        c = src[level]
        below = weight[5, level] * (src[level + 1] - c)
        value = (
            weight[0, level] * c
            + weight[1, level] * roll(c, -1, 0)
            + weight[2, level] * roll(c, 1, 0)
            + weight[3, level] * roll(c, -1, 1)
            + weight[4, level] * roll(c, 1, 1)
            + (below - above)
        )
        return value, below

    for step in range(SUBSTEPS - 1):
        src, dst = (b, a) if step % 2 else (whole if step == 0 else a, b)
        start, stop = step + 1, total - 1 - step

        def body(index, above, src=src, dst=dst, start=start):
            for sub in range(4):
                level = start + 4 * index + sub
                dst[level], above = update(src, level, above)
            return above

        trips = (stop - start) // 4
        above = lax.fori_loop(0, trips, body, edge(src, start - 1))
        for level in range(start + 4 * trips, stop):
            dst[level], above = update(src, level, above)
    src = b if SUBSTEPS % 2 == 0 else a
    outs = (mine_ref, other_ref, send_ref, send_ref)
    for place, out in enumerate(outs):
        block = t ^ place
        first = HALO + HALO * block
        above = edge(src, first - 1)
        tau = None
        for sub in range(HALO):
            value, above = update(src, first + sub, above)
            m = value[:width]
            out[sub + (HALO if place == 3 else 0)] = m
            part = (0.5 + m * m) / levels
            tau = part if tau is None else tau + part
        sums_ref[block] = tau
    zero = jnp.zeros(sums_ref.shape[1:], jnp.float32)

    def thickness(index, *by_comp):
        total = zero
        for holder, part in by_comp:
            total = total + jnp.where((t == 0) & (c == holder), part[index], 0.0)
        return total

    if turn < 3:
        send_ref[2 * HALO] = sum((thickness(index, (turn, sums_ref)) for index in range(4)), zero)
    else:
        running = zero
        for index in range(4):
            if index < 2:
                near_ref[index] = running
            else:
                send_ref[2 * HALO + index - 2] = running
            running = running + thickness(index, *enumerate((*earlier, sums_ref)))


def tau_kernel(*refs):
    sent, received, whole = refs[: len(refs) // 2], refs[len(refs) // 2 : -1], refs[-1]
    _, t = position()
    total = jnp.zeros(whole.shape, jnp.float32)
    for here, there in zip(sent, received):
        total = total + jnp.where(t == 0, here[2 * HALO], jnp.where(t == 2, there[2 * HALO], 0.0))
    whole[...] = total


def gather_kernel(*refs):
    others, across, out = refs[:4], refs[4:6], refs[6]
    depth = others[0].shape[0]
    for index, ref in enumerate(others):
        out[index * depth : (index + 1) * depth] = ref[...]
    for index, ref in enumerate(across):
        out[(4 + index) * depth : (5 + index) * depth] = ref[depth : 2 * depth]


def last_kernel(near, one, two, three, third, fourth, out):
    depth = (out.shape[0] - 1) // 2
    _, t = position()
    out[:depth] = third[depth : 2 * depth]
    out[depth : 2 * depth] = fourth[depth : 2 * depth]
    base = one[...] + two[...] + three[...]
    out[2 * depth] = base + jnp.where(t == 0, near[1], fourth[2 * depth + 1])


def tracer_of(turn, flip):
    c, t = position()
    comps, trcs = lax.axis_size("comp"), lax.axis_size("trc")
    holder = t ^ flip
    return trcs * lax.rem(c + comps - shift_of(turn, holder), comps) + holder


def growth_kernel(terms, react_ref, *refs):
    count, depth, width, _ = refs[-1].shape
    out = refs[-1]
    arrays = max(term[0] for term in terms) + 1
    before = refs[arrays:-1]
    tracers = [tracer_of(turn, flip) for _, _, turn, flip in terms]
    per_level = width // 8

    def chunk(index, carry):
        level = lax.div(index, per_level)
        row = pl.ds(pl.multiple_of(lax.rem(index, per_level) * 8, 8), 8)
        values = [refs[which][start + level, row, :] for which, start, _, _ in terms]
        for i in range(count):
            total = before[0][i, level, row, :] if before else None
            for tracer, value in zip(tracers, values):
                part = react_ref[i, tracer] * value
                total = part if total is None else total + part
            out[i, level, row, :] = total
        return carry

    lax.fori_loop(0, depth * per_level, chunk, 0)


def reaction_kernel(levels, react_ref, sun_ref, near_ref, one, two, three, growth_ref, *refs):
    mine = refs[0:4]
    across = refs[4:8]
    core_ref, last_ref, out_ref, heat_ref, depth, field = refs[8:]
    rows = out_ref.shape[2]
    count = out_ref.shape[0]
    level = pl.program_id(0)
    deep = pl.num_programs(0)
    _, t = position()

    @pl.when(level == 0)
    def _():
        base = one[...] + two[...] + three[...]
        inner = base + jnp.where(t == 0, near_ref[0], across[3][2 * HALO])
        depth[...] = jnp.where(t % 2 == 0, inner, last_ref[2 * deep])

    for turn in range(4):
        field[tracer_of(turn, 0)] = mine[turn][level]
        field[tracer_of(turn, 2)] = across[turn][level]
        field[tracer_of(turn, 1)] = core_ref[turn * deep + level]
        if turn < 2:
            field[tracer_of(turn, 3)] = core_ref[(4 + turn) * deep + level]
        else:
            field[tracer_of(turn, 3)] = last_ref[(turn - 2) * deep + level]
    added = [(tracer_of(2 + part, 3), part) for part in range(2)]

    def chunk(index, carry):
        row = pl.ds(pl.multiple_of(index * 8, 8), 8)
        lead = field[0, row, :]
        tau = (0.5 + lead * lead) / levels
        above = depth[row, :]
        light_top = sun_ref[row, :] * jnp.exp(-above)
        heat_ref[0, row, :] = levels * light_top * (1.0 - jnp.exp(-tau))
        depth[row, :] = above + tau
        light_mid = light_top * jnp.exp(-0.5 * tau)
        limit = light_mid / (light_mid + HALF_LIGHT)
        values = [(tracer, last_ref[part * deep + level, row, :]) for tracer, part in added]
        for i in range(count):
            growth = growth_ref[i, level, row, :]
            for tracer, value in values:
                growth = growth + react_ref[i, tracer] * value
            out_ref[i, 0, row, :] = field[i, row, :] + limit * growth
        return carry

    lax.fori_loop(0, rows // 8, chunk, 0)


def per_device(tracers, eastward, northward, surface_height, sea_mask, mixing, sunlight, reaction):
    i32 = jnp.int32
    depth, width, rows = eastward.shape
    comps, trcs = lax.axis_size("comp"), lax.axis_size("trc")
    tiles = lax.axis_size("horiz")
    levels = depth * comps * trcs
    group = depth * trcs
    tall = group + 2 * HALO
    span = width + 2 * HALO
    forward = [(i, i + 1) for i in range(tiles - 1)]
    backward = [(i + 1, i) for i in range(tiles - 1)]
    flip_x = [(i, i ^ 2) for i in range(trcs)]
    flip_core = [(i, i ^ 1) for i in range(trcs)]
    both = ("comp", "trc")
    edges = 3 * depth + 2

    def ring(*shifts):
        return [
            (trcs * i + j, trcs * ((i + shifts[min(j, len(shifts) - 1)]) % comps) + j)
            for i in range(comps)
            for j in range(trcs)
        ]

    packed = call(
        pack_kernel,
        4,
        out_shape=(local(tall, width, rows),) * 2
        + (local(edges, 8, rows),) * 2
        + (local(levels // 2, 8, rows),) * 2,
        in_specs=[ANY] * 6,
        out_specs=(VMEM,) * 6,
        scratch_shapes=[
            local(levels, 8, rows),
            local(levels, 8, rows),
            pltpu.VMEM((2, 8, rows), i32),
            pltpu.SemaphoreType.DMA((18,)),
        ],
    )(*in_hbm(tracers[0], eastward, northward, mixing, surface_height, sea_mask))
    one, three, low, high, side_low, side_high = packed
    one = lax.ppermute(one, both, ring(1))
    three = lax.ppermute(three, both, ring(2, 3))
    low = lax.ppermute(low, "horiz", forward)
    high = lax.ppermute(high, "horiz", backward)
    side_low = lax.ppermute(side_low, "horiz", forward)
    side_high = lax.ppermute(side_high, "horiz", backward)

    east_out, north_out, flux = call(
        functools.partial(ocean_kernel, levels - 1),
        4,
        out_shape=(array(depth, width, rows),) * 2 + (local(3, depth, span, rows),),
        in_specs=[VMEM] * 7,
        out_specs=(VMEM,) * 3,
    )(eastward, northward, mixing, surface_height, sea_mask, low, high)

    ups = range(comps - 1)
    last, nxt = trcs - 1, trcs
    near = lax.ppermute(
        flux,
        both,
        [(trcs * i + last, trcs * i + nxt + 2) for i in ups] + [(trcs * i + nxt, trcs * i + 1) for i in ups],
    )
    far = lax.ppermute(near, "trc", [(trcs - 2, 0), (1, trcs - 1)])
    across_flux = lax.ppermute(flux, "trc", flip_x)

    whole = local(tall, span, rows)
    flank = local(tall, 8, rows)
    own, side_one, two, side_three = call(
        side_kernel,
        1,
        out_shape=(whole, flank, whole, flank),
        in_specs=[ANY, VMEM, VMEM],
        out_specs=(VMEM,) * 4,
        scratch_shapes=[local(levels, 8, rows), pltpu.SemaphoreType.DMA((6,))],
    )(*in_hbm(tracers[0]), *in_vmem(side_low, side_high))
    side_one = lax.ppermute(side_one, both, ring(1))
    side_three = lax.ppermute(side_three, both, ring(2, 3))
    two = lax.ppermute(two, both, ring(3, 2))
    parts = ((own,), (one, side_one), (three, side_three), (two,))
    pair = call(
        pair_kernel,
        1,
        out_shape=local(2, 3, depth, span, rows),
        in_specs=[VMEM] * 2,
        out_specs=VMEM,
    )(*in_vmem(flux, across_flux))
    core_flux = lax.ppermute(pair, "trc", flip_core)
    rim = call(
        rim_kernel, 1, out_shape=local(3, depth, span, rows), in_specs=[VMEM] * 2, out_specs=VMEM
    )(*in_vmem(near, far))
    core_rim = lax.ppermute(rim, "trc", flip_core)
    weight = local(6, tall, span, rows)
    weight_inner = call(
        weight_kernel, 2, out_shape=weight, in_specs=[VMEM] * 2, out_specs=VMEM
    )(*in_vmem(pair, core_flux))
    weight = call(
        weight_kernel,
        1,
        out_shape=weight,
        in_specs=[VMEM] * 3,
        out_specs=VMEM,
        input_output_aliases={0: 0},
    )(*in_vmem(weight_inner, rim, core_rim))
    piece = local(depth, width, rows)
    mine, other, sends, across, sums = [], [], [], [], []
    for turn in range(4):
        inputs = [weight, *parts[turn]]
        sent = 2 * depth
        if turn == 3:
            inputs += sums
        sent += 2 if turn == 3 else 1
        results = call(
            functools.partial(transport_kernel, levels, turn),
            6,
            out_shape=(local(2, width, rows),) * (turn == 3)
            + (piece, piece, local(sent, width, rows), piece),
            in_specs=[VMEM] * len(inputs),
            out_specs=(VMEM,) * (5 if turn == 3 else 4),
            scratch_shapes=[local(tall, span, rows)] * 2,
        )(*in_vmem(*inputs))
        m, o, held, total = results[-4:]
        mine.append(m)
        other.append(o)
        sends.append(held)
        across.append(lax.ppermute(held, "trc", flip_x))
        sums.append(total)
    near = results[0]
    bases = []
    for k in range(1, comps):
        known = comps - k
        thick = call(
            tau_kernel,
            1,
            out_shape=local(width, rows),
            in_specs=[VMEM] * (2 * known),
            out_specs=VMEM,
        )(*in_vmem(*sends[:known], *across[:known]))
        bases.append(lax.ppermute(thick, "comp", [(i, i + k) for i in range(comps - k)]))
    count = reaction.shape[0]

    def grow(terms, arrays, before=()):
        return call(
            functools.partial(growth_kernel, terms),
            4,
            out_shape=local(count, depth, width, rows),
            in_specs=[SMEM] + [VMEM] * (len(arrays) + len(before)),
            out_specs=VMEM,
        )(reaction, *in_vmem(*arrays, *before))

    cross = call(
        gather_kernel,
        2,
        out_shape=local(6 * depth, width, rows),
        in_specs=[VMEM] * 6,
        out_specs=VMEM,
    )(*in_vmem(*other, *across[:2]))
    cross = lax.ppermute(cross, "trc", flip_core)
    growth = grow(
        tuple((i, 0, i, 0) for i in range(4)) + tuple((4 + i, 0, i, 2) for i in range(2)),
        (*mine, *across[:2]),
    )
    growth = grow(
        tuple((0, i * depth, i, 1) for i in range(4)) + tuple((0, (4 + i) * depth, i, 3) for i in range(2)),
        (cross,),
        (growth,),
    )
    final = call(
        last_kernel,
        1,
        out_shape=local(2 * depth + 1, width, rows),
        in_specs=[VMEM] * 6,
        out_specs=VMEM,
    )(*in_vmem(near, *bases, *across[2:]))
    final = lax.ppermute(final, "trc", flip_core)
    growth = grow(((0, 0, 2, 2), (1, 0, 3, 2)), tuple(across[2:]), (growth,))
    tracers_out, heating = call(
        functools.partial(reaction_kernel, levels),
        6,
        grid=(depth,),
        out_shape=(array(count, depth, width, rows), array(depth, width, rows)),
        in_specs=[SMEM] + [VMEM] * 16,
        out_specs=(
            pl.BlockSpec((count, 1, width, rows), lambda l: (0, l, 0, 0)),
            pl.BlockSpec((1, width, rows), lambda l: (l, 0, 0)),
        ),
        scratch_shapes=[local(width, rows), local(count, width, rows)],
    )(reaction, *in_vmem(sunlight, near, *bases, growth, *mine, *across, cross, final))
    return (east_out, north_out, tracers_out, heating)


def solution(mesh):
    return jax.shard_map(
        per_device,
        mesh=mesh,
        in_specs=(
            P(("comp", "trc"), None, "horiz", None),
            P(("comp", "trc"), "horiz", None),
            P(("comp", "trc"), "horiz", None),
            P("horiz", None),
            P("horiz", None),
            P(("comp", "trc"), "horiz", None),
            P("horiz", None),
            P(),
        ),
        out_specs=(
            P(("comp", "trc"), "horiz", None),
            P(("comp", "trc"), "horiz", None),
            P(None, ("comp", "trc"), "horiz", None),
            P(("comp", "trc"), "horiz", None),
        ),
        check_vma=False,
    )
```
